32 devices in a mesh: grp: 2 (over y), row: 4 (over x, core), col: 4 (over z).
Axes of the slice: x: 2, y: 2, z: 4, core: 2. Of those that a mesh axis runs over, the one named last changes fastest.
Arguments:
- factor: float32 [8, 4, 768, 768], P(('grp', 'row'), 'col'), parts along dimension 0
- rhs: float32 [8, 768, 64], P(('grp', 'row')), parts along dimension 0, may hold values from -6 to 6
- pattern: int32 [8, 4], P('grp'), parts along dimension 0, may hold values from 0 to 1, as said below
Outputs:
- solution: float32 [8, 768, 64], P(('grp', 'col'), 'row'), parts along dimension 0
The draws below stay inside these ranges and needn't reach their ends.
There are 2 independent parts, one for each index of `grp`. The reference program is written for one: setup_inputs(seed, part) draws one part's arguments, and reference() takes and returns one part's arrays. A program takes and returns all parts, laid end to end along the dimension named above; each array names one. Nothing has to cross between parts.
Inputs may be any that keep to these rules, and one draw needn't show every extreme that they name: pattern[i, j] = 1 only where j < i; the blocks form an elimination tree in which every block but the last has exactly one parent p > j with pattern[p, j] = 1, and pattern[i, j] = 1 only where i is an ancestor of j; every chain of blocks linked by pattern has at most 4 blocks and some chain has exactly 4.
All inputs are finite; a program needn't handle non-finite values.
Results may differ from the reference program's by a relative error of at most 0.0001.
Values sent between devices are 32-bit elements; how exact they have to be, the bound alone decides.
A program may use at most 64 MiB of HBM per device.

```python
import jax
import jax.numpy as jnp
from jax import lax

TILE = 768
RHS = 64
BLOCKS = 4
LEVELS = 4


def draw_factor(key, part):
    key_base, key_diag = jax.random.split(jax.random.fold_in(key, 11))
    shape_all = (BLOCKS, BLOCKS, TILE, TILE)
    base = jax.random.normal(key_base, shape_all, jnp.float32)
    diag_values = jnp.exp(jax.random.uniform(key_diag, (BLOCKS, 1, TILE, 1), jnp.float32, jnp.log(0.5), jnp.log(2.0)))
    identity = jnp.eye(TILE, dtype=jnp.float32)
    on_diagonal = (jnp.arange(BLOCKS)[:, None] == jnp.arange(BLOCKS)[None, :])[:, :, None, None]
    dominant = base * (0.5 / jnp.sqrt(TILE * 1.0)) + diag_values * identity
    return jnp.where(on_diagonal, dominant, base / jnp.sqrt(8.0 * TILE))


def draw_pattern(key, part):
    key_parent, key_bits = jax.random.split(jax.random.fold_in(key, 7))
    indices = jnp.arange(BLOCKS, dtype=jnp.int32)
    spine_start = BLOCKS - LEVELS
    leaf_parent = spine_start + jax.random.randint(key_parent, (BLOCKS,), 1, LEVELS, dtype=jnp.int32)
    parents = jnp.where(indices >= spine_start, indices + 1, leaf_parent)
    position = jnp.where(indices >= spine_start, indices - spine_start, leaf_parent - spine_start - 1)
    ancestor = (indices[:, None] >= spine_start) & (indices[:, None] - spine_start > position[None, :])
    random_bits = jax.random.randint(key_bits, (BLOCKS, BLOCKS), 0, 2, dtype=jnp.int32)
    is_parent = indices[:, None] == parents[None, :]
    return jnp.where(ancestor, jnp.where(is_parent, 1, random_bits), 0).astype(jnp.int32)


def steps_of(own_key, shape, pieces, smallest, high):
    loudness = 1.0
    for axis_at, parts in pieces:
        draws = jax.random.uniform(jax.random.fold_in(jax.random.fold_in(own_key, 6), axis_at), (parts,), jnp.float32, smallest / len(pieces), high / len(pieces))
        loudness = loudness * jnp.repeat(jnp.exp(draws), shape[axis_at] // parts).reshape((-1,) + (1,) * (len(shape) - 1 - axis_at))
    return loudness


def normal_values(stream_key, shape, deviation, reach, cuts=(), kind=jnp.bfloat16):
    level = steps_of(stream_key, shape, cuts, -0.22, 0.18) if cuts else 1.0
    entries = jax.random.normal(stream_key, shape, jnp.float32) * deviation * level
    return jnp.minimum(jnp.maximum(entries, -reach), reach).astype(kind)


def setup_inputs(seed: int = 0, part: int = 0) -> dict:
    key_list = jax.random.split(jax.random.key(seed), 4)
    part_keys = jax.random.split(jax.random.fold_in(key_list[3], part), 4)
    return {
        "factor": draw_factor(jax.random.fold_in(jax.random.fold_in(key_list[3], part), 71), part),
        "rhs": normal_values(part_keys[1], (BLOCKS, TILE, RHS), 1.0, 6.0, ((0, 4),), jnp.float32),
        "pattern": draw_pattern(jax.random.fold_in(jax.random.fold_in(key_list[3], part), 71), part),
    }


def reference(factor, rhs, pattern):
    solved = jnp.zeros((BLOCKS, TILE, RHS), jnp.float32)
    for block_index in range(BLOCKS):
        weights = (pattern[block_index] == 1).astype(jnp.float32)
        carried = jnp.einsum("jab,jbr->ar", factor[block_index], solved * weights[:, None, None], precision=lax.Precision.HIGHEST)
        answer = jnp.dot(factor[block_index, block_index], rhs[block_index] - carried, precision=lax.Precision.HIGHEST, preferred_element_type=jnp.float32)
        solved = solved.at[block_index].set(answer)
    return solved
```

```python
import functools

import jax
import jax.numpy as jnp
from jax import lax
from jax.experimental import pallas as pl
from jax.experimental.pallas import tpu as pltpu
from jax.sharding import PartitionSpec as P

MESH = pl.DeviceIdType.MESH
BF = jnp.bfloat16
F32 = jnp.float32


def low_lanes(shape, half):
    return lax.broadcasted_iota(jnp.int32, shape, 1) < half


def halves(packed, half):
    low = low_lanes(packed.shape, half)
    lead = packed.astype(BF).astype(F32)
    rest = packed - lead
    upper = jnp.where(low, lead, pltpu.roll(rest, half, 1))
    lower = jnp.where(low, pltpu.roll(lead, half, 1), rest)
    return upper.astype(BF), lower.astype(BF)


def kernel(
    n, size, step, half,
    factor, rhs, pattern, out,
    a32, ahi, alo, right, w, acc, both, sent, xin, pin, piece, pin_slice,
    a_sem, r_sem, x_send, x_recv, p_send, p_recv, s_send, s_recv,
):
    r = lax.axis_index("row")
    c = lax.axis_index("col")
    chunks = size // step
    mid = step // 2
    own = size // n
    bit = own // 2
    diag = r == c
    lower = r > c
    active = r >= c

    def load(k):
        rows = pl.ds(k * step, step)
        return pltpu.make_async_copy(factor.at[0, 0, rows, :], a32.at[rows, :], a_sem.at[k])

    def load_right():
        return pltpu.make_async_copy(rhs.at[0], right, r_sem)

    @pl.when(active)
    def _():
        for k in range(chunks):
            load(k).start()

    @pl.when(diag)
    def _():
        load_right().start()

    barrier = pltpu.get_barrier_semaphore()
    for i in range(n):
        @pl.when(diag & (i < r))
        def _():
            pl.semaphore_signal(barrier, inc=1, device_id={"col": i}, device_id_type=MESH)

    @pl.when(jnp.logical_not(diag))
    def _():
        pl.semaphore_signal(barrier, inc=1, device_id={"row": c}, device_id_type=MESH)

    @pl.when(active)
    def _():
        keep = jnp.where(diag | (pattern[r, c] == 1), 1.0, 0.0).astype(F32)
        block = 64
        for k in range(chunks):
            load(k).wait()

            def split(t, carry):
                rows = pl.ds(pl.multiple_of(k * step + t * block, block), block)
                full = a32[rows, :] * keep
                lead = full.astype(BF)
                ahi[rows, :] = lead
                alo[rows, :] = (full - lead.astype(F32)).astype(BF)
                return carry

            lax.fori_loop(0, step // block, split, 0)

    @pl.when(diag)
    def _():
        load_right().wait()
        pl.semaphore_wait(barrier, n - 1)

    @pl.when(lower)
    def _():
        pl.semaphore_wait(barrier, 1)

    def x_copy(i, m):
        return pltpu.make_async_remote_copy(
            src_ref=sent.at[m], dst_ref=xin.at[m], send_sem=x_send.at[i, m], recv_sem=x_recv.at[m],
            device_id={"row": i}, device_id_type=MESH,
        )

    def p_copy(m):
        return pltpu.make_async_remote_copy(
            src_ref=sent.at[m], dst_ref=pin.at[c, m], send_sem=p_send.at[m], recv_sem=p_recv.at[c, m],
            device_id={"col": r}, device_id_type=MESH,
        )

    def p_arrival(j, m):
        return pltpu.make_async_remote_copy(
            src_ref=sent.at[m], dst_ref=pin.at[j, m], send_sem=p_send.at[m], recv_sem=p_recv.at[j, m],
            device_id={"col": r}, device_id_type=MESH,
        )

    def s_copy(i):
        return pltpu.make_async_remote_copy(
            src_ref=piece.at[i], dst_ref=pin_slice, send_sem=s_send.at[i], recv_sem=s_recv,
            device_id={"row": i}, device_id_type=MESH,
        )

    def place(value):
        out[0, :bit, :] = value[:, :half]
        out[0, bit:, :] = pltpu.roll(value, half, 1)[:, :half]

    @pl.when(diag)
    def _():
        for k in range(chunks):
            base = k * step
            xin[k] = jnp.concatenate(
                [right[base:base + mid, :], right[base + mid:base + step, :]], axis=1
            )

    @pl.when(active)
    def _():
        for k in range(chunks):
            base = k * step

            @pl.when(lower)
            def _():
                x_copy(0, k).wait_recv()

            for j in range(n - 1):
                @pl.when(diag & (j < r))
                def _():
                    p_arrival(j, k).wait_recv()
                    xin[k] = xin[k] - pin[j, k]

            first, second = halves(xin[k], half)
            w[base:base + mid, :] = first
            w[base + mid:base + step, :] = second
            last = k == chunks - 1
            for m in range(chunks):
                rows = slice(m * step, (m + 1) * step)
                cols = slice(base, base + step)
                part = jnp.dot(ahi[rows, cols], w[cols, :], preferred_element_type=F32)
                part += jnp.dot(alo[rows, cols], w[cols, :], preferred_element_type=F32)
                if k:
                    part += acc[rows, :]
                if not last:
                    acc[rows, :] = part
                    continue
                part = part + pltpu.roll(part, half, 1)
                both[rows, :] = part
                sent[m] = jnp.where(low_lanes((mid, 2 * half), half), part[:mid], part[mid:])

                @pl.when(lower)
                def _():
                    p_copy(m).start()

                for i in range(1, n):
                    @pl.when(diag & (i > r))
                    def _():
                        x_copy(i, m).start()

    @pl.when(diag)
    def _():
        for i in range(n):
            top = both[i * own:i * own + bit, :]
            bottom = both[i * own + bit:(i + 1) * own, :]
            value = jnp.where(low_lanes((bit, 2 * half), half), top, bottom)
            piece[i] = value

            @pl.when(i != r)
            def _():
                s_copy(i).start()

            @pl.when(i == r)
            def _():
                place(value)

    @pl.when(jnp.logical_not(diag))
    def _():
        s_copy(0).wait_recv()
        place(pin_slice[...])

    @pl.when(lower)
    def _():
        for m in range(chunks):
            p_copy(m).wait_send()

    for i in range(n):
        @pl.when(diag & (i > r))
        def _():
            for m in range(chunks):
                x_copy(i, m).wait_send()

        @pl.when(diag & (i != r))
        def _():
            s_copy(i).wait_send()


def local(n, factor, rhs, pattern):
    size, columns = rhs.shape[1], rhs.shape[2]
    step = 256 if size % 256 == 0 else size
    chunks = size // step
    half = columns
    own = size // n
    dma = pltpu.SemaphoreType.DMA
    return pl.pallas_call(
        functools.partial(kernel, n, size, step, half),
        out_shape=jax.ShapeDtypeStruct((1, own, columns), F32),
        in_specs=[
            pl.BlockSpec(memory_space=pl.ANY),
            pl.BlockSpec(memory_space=pl.ANY),
            pl.BlockSpec(memory_space=pltpu.SMEM),
        ],
        out_specs=pl.BlockSpec(memory_space=pltpu.VMEM),
        scratch_shapes=[
            pltpu.VMEM((size, size), F32),
            pltpu.VMEM((size, size), BF),
            pltpu.VMEM((size, size), BF),
            pltpu.VMEM((size, columns), F32),
            pltpu.VMEM((size, 2 * half), BF),
            pltpu.VMEM((size, 2 * half), F32),
            pltpu.VMEM((size, 2 * half), F32),
            pltpu.VMEM((chunks, step // 2, 2 * half), F32),
            pltpu.VMEM((chunks, step // 2, 2 * half), F32),
            pltpu.VMEM((n - 1, chunks, step // 2, 2 * half), F32),
            pltpu.VMEM((n, own // 2, 2 * half), F32),
            pltpu.VMEM((own // 2, 2 * half), F32),
            dma((chunks,)),
            dma,
            dma((n, chunks)),
            dma((chunks,)),
            dma((chunks,)),
            dma((n - 1, chunks)),
            dma((n,)),
            dma,
        ],
        compiler_params=pltpu.CompilerParams(
            collective_id=0, has_side_effects=True, vmem_limit_bytes=40 * 1024 * 1024
        ),
    )(factor, rhs, pattern)


def solution(mesh):
    in_specs = (P(("grp", "row"), "col", None, None), P(("grp", "row"), None, None), P("grp", None))
    out_specs = P(("grp", "col"), "row", None)
    return jax.shard_map(
        functools.partial(local, mesh.shape["row"]),
        mesh=mesh, in_specs=in_specs, out_specs=out_specs, check_vma=False,
    )
```

```python
import functools

import jax
import jax.numpy as jnp
from jax import lax
from jax.experimental import pallas as pl
from jax.experimental.pallas import tpu as pltpu
from jax.sharding import PartitionSpec as P

MESH = pl.DeviceIdType.MESH
BF = jnp.bfloat16
F32 = jnp.float32


def low_lanes(shape, half):
    return lax.broadcasted_iota(jnp.int32, shape, 1) < half


def halves(packed, half):
    low = low_lanes(packed.shape, half)
    lead = packed.astype(BF).astype(F32)
    rest = packed - lead
    upper = jnp.where(low, lead, pltpu.roll(rest, half, 1))
    lower = jnp.where(low, pltpu.roll(lead, half, 1), rest)
    return upper.astype(BF), lower.astype(BF)


def kernel(
    n, size, step, half,
    factor, rhs, pattern, out,
    links, a32, ahi, alo, right, w, acc, both, sent, xin, pin, piece, pin_slice,
    a_sem, r_sem, l_sem, x_send, x_recv, p_send, p_recv, s_send, s_recv,
):
    r = lax.axis_index("row")
    c = lax.axis_index("col")
    chunks = size // step
    mid = step // 2
    own = size // n
    bit = own // 2
    diag = r == c
    lower = r > c
    active = r >= c

    def load(k):
        rows = pl.ds(k * step, step)
        return pltpu.make_async_copy(factor.at[0, 0, rows, :], a32.at[rows, :], a_sem.at[k])

    def load_right():
        return pltpu.make_async_copy(rhs.at[0], right, r_sem)

    def load_links():
        return pltpu.make_async_copy(pattern, links, l_sem)

    @pl.when(active)
    def _():
        load_links().start()

    @pl.when(diag)
    def _():
        load_right().start()

    @pl.when(active)
    def _():
        for k in range(chunks):
            load(k).start()

    barrier = pltpu.get_barrier_semaphore()
    for i in range(n):
        @pl.when(diag & (i < r))
        def _():
            pl.semaphore_signal(barrier, inc=1, device_id={"col": i}, device_id_type=MESH)

    @pl.when(jnp.logical_not(diag))
    def _():
        pl.semaphore_signal(barrier, inc=1, device_id={"row": c}, device_id_type=MESH)

    block = 64

    def prepare(k, keep):
        load(k).wait()

        def split(t, carry):
            rows = pl.ds(pl.multiple_of(k * step + t * block, block), block)
            full = a32[rows, :] * keep
            lead = full.astype(BF)
            ahi[rows, :] = lead
            alo[rows, :] = (full - lead.astype(F32)).astype(BF)
            return carry

        lax.fori_loop(0, step // block, split, 0)

    def x_copy(i, m):
        return pltpu.make_async_remote_copy(
            src_ref=sent.at[m], dst_ref=xin.at[m], send_sem=x_send.at[i, m], recv_sem=x_recv.at[m],
            device_id={"row": i}, device_id_type=MESH,
        )

    def p_copy(m):
        return pltpu.make_async_remote_copy(
            src_ref=sent.at[m], dst_ref=pin.at[c, m], send_sem=p_send.at[m], recv_sem=p_recv.at[c, m],
            device_id={"col": r}, device_id_type=MESH,
        )

    def p_arrival(j, m):
        return pltpu.make_async_remote_copy(
            src_ref=sent.at[m], dst_ref=pin.at[j, m], send_sem=p_send.at[m], recv_sem=p_recv.at[j, m],
            device_id={"col": r}, device_id_type=MESH,
        )

    def s_copy(i):
        return pltpu.make_async_remote_copy(
            src_ref=piece.at[i], dst_ref=pin_slice, send_sem=s_send.at[i], recv_sem=s_recv,
            device_id={"row": i}, device_id_type=MESH,
        )

    def place(value):
        turned = value.T
        out[0, :, :bit] = turned[:half]
        out[0, :, bit:] = turned[half:]

    def weave(k):
        first, second = halves(xin[k], half)
        w[k * step:k * step + mid, :] = first
        w[k * step + mid:(k + 1) * step, :] = second

    def product(rows, cols):
        part = jnp.dot(ahi[rows, cols], w[cols, :], preferred_element_type=F32)
        return part + jnp.dot(alo[rows, cols], w[cols, :], preferred_element_type=F32)

    def finish(m, part):
        part = part + pltpu.roll(part, half, 1)
        both[m * step:(m + 1) * step, :] = part
        sent[m] = jnp.where(low_lanes((mid, 2 * half), half), part[:mid], part[mid:])

    @pl.when(diag)
    def _():
        load_right().wait()
        for k in range(chunks):
            base = k * step
            xin[k] = jnp.concatenate(
                [right[:, base:base + mid], right[:, base + mid:base + step]], axis=0
            ).T

    @pl.when(active)
    def _():
        load_links().wait()

    @pl.when(diag & (r == 0))
    def _():
        for k in range(chunks):
            weave(k)
        for m in range(chunks):
            prepare(m, jnp.float32(1.0))
            finish(m, product(slice(m * step, (m + 1) * step), slice(0, size)))
            if m == 0:
                pl.semaphore_wait(barrier, n - 1)
            x_copy(1, m).start()

    @pl.when(active & (r > 0))
    def _():
        keep = jnp.where(diag | (links[r, c] == 1), 1.0, 0.0).astype(F32)
        for k in range(chunks):
            prepare(k, keep)

        @pl.when(diag)
        def _():
            pl.semaphore_wait(barrier, n - 1)

        @pl.when(lower)
        def _():
            pl.semaphore_wait(barrier, 1)

        for k in range(chunks):
            base = k * step

            @pl.when(lower)
            def _():
                x_copy(0, k).wait_recv()

            for j in range(n - 1):
                @pl.when(diag & (j < r))
                def _():
                    p_arrival(j, k).wait_recv()
                    xin[k] = xin[k] - pin[j, k]

            weave(k)
            last = k == chunks - 1
            for m in range(chunks):
                rows = slice(m * step, (m + 1) * step)
                part = product(rows, slice(base, base + step))
                if k:
                    part += acc[rows, :]
                if not last:
                    acc[rows, :] = part
                    continue
                finish(m, part)

                @pl.when(lower)
                def _():
                    p_copy(m).start()

                for i in range(2, n):
                    @pl.when(diag & (i == r + 1))
                    def _():
                        x_copy(i, m).start()

    for i in range(2, n):
        @pl.when(diag & (i > r + 1))
        def _():
            for m in range(chunks):
                x_copy(i, m).start()

    @pl.when(diag)
    def _():
        for i in range(n):
            top = both[i * own:i * own + bit, :]
            bottom = both[i * own + bit:(i + 1) * own, :]
            value = jnp.where(low_lanes((bit, 2 * half), half), top, bottom)
            piece[i] = value

            @pl.when(i != r)
            def _():
                s_copy(i).start()

            @pl.when(i == r)
            def _():
                place(value)

    @pl.when(jnp.logical_not(diag))
    def _():
        s_copy(0).wait_recv()
        place(pin_slice[...])

    @pl.when(lower)
    def _():
        for m in range(chunks):
            p_copy(m).wait_send()

    for i in range(n):
        @pl.when(diag & (i > r))
        def _():
            for m in range(chunks):
                x_copy(i, m).wait_send()

        @pl.when(diag & (i != r))
        def _():
            s_copy(i).wait_send()


def local(n, factor, rhs, pattern):
    size, columns = rhs.shape[1], rhs.shape[2]
    step = 256 if size % 256 == 0 else size
    chunks = size // step
    half = columns
    own = size // n
    dma = pltpu.SemaphoreType.DMA
    solved = pl.pallas_call(
        functools.partial(kernel, n, size, step, half),
        out_shape=jax.ShapeDtypeStruct((1, columns, own), F32),
        in_specs=[
            pl.BlockSpec(memory_space=pltpu.HBM),
            pl.BlockSpec(memory_space=pltpu.HBM),
            pl.BlockSpec(memory_space=pltpu.HBM),
        ],
        out_specs=pl.BlockSpec(memory_space=pltpu.VMEM),
        scratch_shapes=[
            pltpu.SMEM(pattern.shape, jnp.int32),
            pltpu.VMEM((size, size), F32),
            pltpu.VMEM((size, size), BF),
            pltpu.VMEM((size, size), BF),
            pltpu.VMEM((columns, size), F32),
            pltpu.VMEM((size, 2 * half), BF),
            pltpu.VMEM((size, 2 * half), F32),
            pltpu.VMEM((size, 2 * half), F32),
            pltpu.VMEM((chunks, step // 2, 2 * half), F32),
            pltpu.VMEM((chunks, step // 2, 2 * half), F32),
            pltpu.VMEM((n - 1, chunks, step // 2, 2 * half), F32),
            pltpu.VMEM((n, own // 2, 2 * half), F32),
            pltpu.VMEM((own // 2, 2 * half), F32),
            dma((chunks,)),
            dma,
            dma,
            dma((n, chunks)),
            dma((chunks,)),
            dma((chunks,)),
            dma((n - 1, chunks)),
            dma((n,)),
            dma,
        ],
        compiler_params=pltpu.CompilerParams(
            collective_id=0, has_side_effects=True, vmem_limit_bytes=40 * 1024 * 1024
        ),
    )(*[pltpu.with_memory_space_constraint(v, pltpu.HBM) for v in (factor, jnp.swapaxes(rhs, 1, 2), pattern)])
    return jnp.swapaxes(solved, 1, 2)


def solution(mesh):
    in_specs = (P(("grp", "row"), "col", None, None), P(("grp", "row"), None, None), P("grp", None))
    out_specs = P(("grp", "col"), "row", None)
    return jax.shard_map(
        functools.partial(local, mesh.shape["row"]),
        mesh=mesh, in_specs=in_specs, out_specs=out_specs, check_vma=False,
    )
```

```python
import functools

import jax
import jax.numpy as jnp
from jax import lax
from jax.experimental import pallas as pl
from jax.experimental.pallas import tpu as pltpu
from jax.sharding import PartitionSpec as P

MESH = pl.DeviceIdType.MESH
BF = jnp.bfloat16
F32 = jnp.float32


def low_lanes(shape, half):
    return lax.broadcasted_iota(jnp.int32, shape, 1) < half


def halves(packed, half):
    low = low_lanes(packed.shape, half)
    lead = packed.astype(BF).astype(F32)
    rest = packed - lead
    upper = jnp.where(low, lead, pltpu.roll(rest, half, 1))
    lower = jnp.where(low, pltpu.roll(lead, half, 1), rest)
    return upper.astype(BF), lower.astype(BF)


def kernel(
    n, size, step, half,
    factor, rhs, pattern, out,
    links, a32, ahi, alo, right, w, acc, both, sent, xin, pin, piece, pin_slice, d32, dhi, dlo,
    a_sem, r_sem, l_sem, x_send, x_recv, p_send, p_recv, s_send, s_recv, d_send, d_recv, p_send2,
):
    r = lax.axis_index("row")
    c = lax.axis_index("col")
    chunks = size // step
    mid = step // 2
    own = size // n
    bit = own // 2
    diag = r == c
    lower = r > c
    active = r >= c
    helper = (r == n - 1) & (c == n - 2)
    final = (r == n - 1) & (c == n - 1)
    early = n // 2
    from_helper = (c == n - 1) & (r < early)

    def load(k):
        rows = pl.ds(k * step, step)
        return pltpu.make_async_copy(factor.at[0, 0, rows, :], a32.at[rows, :], a_sem.at[k])

    def load_right():
        return pltpu.make_async_copy(rhs.at[0], right, r_sem)

    def load_links():
        return pltpu.make_async_copy(pattern, links, l_sem)

    @pl.when(active)
    def _():
        load_links().start()

    @pl.when(diag | helper)
    def _():
        load_right().start()

    @pl.when(active)
    def _():
        for k in range(chunks):
            load(k).start()

    barrier = pltpu.get_barrier_semaphore()
    for i in range(n):
        @pl.when(diag & (i < r))
        def _():
            pl.semaphore_signal(barrier, inc=1, device_id={"col": i}, device_id_type=MESH)

    @pl.when(jnp.logical_not(diag) & jnp.logical_not(from_helper))
    def _():
        pl.semaphore_signal(barrier, inc=1, device_id={"row": c}, device_id_type=MESH)

    @pl.when(from_helper)
    def _():
        pl.semaphore_signal(
            barrier, inc=1, device_id={"row": n - 1, "col": n - 2}, device_id_type=MESH
        )

    @pl.when(helper)
    def _():
        for j in range(n):
            if j != n - 2:
                pl.semaphore_signal(barrier, inc=1, device_id={"col": j}, device_id_type=MESH)

    block = 64
    part_rows = early * own // 2

    def prepare(k, keep):
        load(k).wait()

        def split(t, carry):
            rows = pl.ds(pl.multiple_of(k * step + t * block, block), block)
            full = a32[rows, :] * keep
            lead = full.astype(BF)
            ahi[rows, :] = lead
            alo[rows, :] = (full - lead.astype(F32)).astype(BF)
            return carry

        lax.fori_loop(0, step // block, split, 0)

    def x_copy(i, m):
        return pltpu.make_async_remote_copy(
            src_ref=sent.at[m], dst_ref=xin.at[m], send_sem=x_send.at[i, m], recv_sem=x_recv.at[m],
            device_id={"row": i}, device_id_type=MESH,
        )

    def p_copy(m):
        return pltpu.make_async_remote_copy(
            src_ref=sent.at[m], dst_ref=pin.at[c, m], send_sem=p_send.at[m], recv_sem=p_recv.at[c, m],
            device_id={"col": r}, device_id_type=MESH,
        )

    def p_arrival(j, m):
        return pltpu.make_async_remote_copy(
            src_ref=sent.at[m], dst_ref=pin.at[j, m], send_sem=p_send.at[m], recv_sem=p_recv.at[j, m],
            device_id={"col": r}, device_id_type=MESH,
        )

    def h_copy(m):
        return pltpu.make_async_remote_copy(
            src_ref=sent.at[m], dst_ref=pin.at[c, m], send_sem=p_send2.at[m], recv_sem=p_recv.at[c, m],
            device_id={"col": n - 2}, device_id_type=MESH,
        )

    def d_copy(q):
        rows = pl.ds(q * part_rows, part_rows)
        return pltpu.make_async_remote_copy(
            src_ref=factor.at[0, 0, rows, :], dst_ref=d32.at[rows, :],
            send_sem=d_send.at[q], recv_sem=d_recv.at[q],
            device_id={"col": n - 2}, device_id_type=MESH,
        )

    def e_copy(i):
        return pltpu.make_async_remote_copy(
            src_ref=piece.at[i], dst_ref=pin_slice, send_sem=s_send.at[i], recv_sem=s_recv,
            device_id={"row": i, "col": n - 1}, device_id_type=MESH,
        )

    def s_copy(i):
        return pltpu.make_async_remote_copy(
            src_ref=piece.at[i], dst_ref=pin_slice, send_sem=s_send.at[i], recv_sem=s_recv,
            device_id={"row": i}, device_id_type=MESH,
        )

    def place(value):
        turned = value.T
        out[0, :, :bit] = turned[:half]
        out[0, :, bit:] = turned[half:]

    def weave(k, value):
        first, second = halves(value, half)
        w[k * step:k * step + mid, :] = first
        w[k * step + mid:(k + 1) * step, :] = second

    def product(rows, cols):
        part = jnp.dot(ahi[rows, cols], w[cols, :], preferred_element_type=F32)
        return part + jnp.dot(alo[rows, cols], w[cols, :], preferred_element_type=F32)

    def finish(m, part):
        part = part + pltpu.roll(part, half, 1)
        both[m * step:(m + 1) * step, :] = part
        sent[m] = jnp.where(low_lanes((mid, 2 * half), half), part[:mid], part[mid:])

    def right_chunk(k):
        base = k * step
        return jnp.concatenate(
            [right[:, base:base + mid], right[:, base + mid:base + step]], axis=0
        ).T

    @pl.when(diag | helper)
    def _():
        load_right().wait()

    @pl.when(diag)
    def _():
        for k in range(chunks):
            xin[k] = right_chunk(k)

    @pl.when(active)
    def _():
        load_links().wait()

    @pl.when(diag & (r == 0))
    def _():
        for k in range(chunks):
            weave(k, xin[k])
        for m in range(chunks):
            prepare(m, jnp.float32(1.0))
            finish(m, product(slice(m * step, (m + 1) * step), slice(0, size)))
            if m == 0:
                pl.semaphore_wait(barrier, n - 1)
            x_copy(1, m).start()

    @pl.when(active & (r > 0))
    def _():
        keep = jnp.where(diag | (links[r, c] == 1), 1.0, 0.0).astype(F32)

        @pl.when(final)
        def _():
            pl.semaphore_wait(barrier, n - early)
            for q in range(2):
                d_copy(q).start()

        for k in range(chunks):
            prepare(k, keep)

        @pl.when(diag & (r < n - 1))
        def _():
            pl.semaphore_wait(barrier, n - 1)

        @pl.when(lower & (r < n - 1))
        def _():
            pl.semaphore_wait(barrier, 1)

        @pl.when(lower & (r == n - 1) & (c < n - 2))
        def _():
            pl.semaphore_wait(barrier, 2)

        @pl.when(helper)
        def _():
            pl.semaphore_wait(barrier, 1 + early)
            for q in range(2):
                d_copy(q).wait_recv()
            strip = 16

            def split(t, carry):
                rows = pl.ds(pl.multiple_of(t * strip, strip), strip)
                full = d32[rows, :]
                lead = full.astype(BF)
                dhi[rows, :] = lead
                dlo[rows, :] = (full - lead.astype(F32)).astype(BF)
                return carry

            lax.fori_loop(0, early * own // strip, split, 0)

        for k in range(chunks):
            base = k * step

            @pl.when(lower)
            def _():
                x_copy(0, k).wait_recv()

            for j in range(n - 1):
                @pl.when(diag & (j < r))
                def _():
                    p_arrival(j, k).wait_recv()
                    xin[k] = xin[k] - pin[j, k]

            weave(k, xin[k])
            last = k == chunks - 1
            for m in range(chunks):
                rows = slice(m * step, (m + 1) * step)
                part = product(rows, slice(base, base + step))
                if k:
                    part += acc[rows, :]
                if not last:
                    acc[rows, :] = part
                    continue
                finish(m, part)

                @pl.when(lower)
                def _():
                    p_copy(m).start()

                @pl.when((r == n - 1) & (c < n - 2))
                def _():
                    h_copy(m).start()

                for i in range(2, n):
                    @pl.when(diag & (i == r + 1))
                    def _():
                        x_copy(i, m).start()

    for i in range(2, n):
        @pl.when(diag & (i > r + 1))
        def _():
            for m in range(chunks):
                x_copy(i, m).start()

    @pl.when(helper)
    def _():
        for k in range(chunks):
            value = right_chunk(k) - sent[k]
            for j in range(n - 2):
                p_arrival(j, k).wait_recv()
                value = value - pin[j, k]
            weave(k, value)
        for i in range(early):
            rows = slice(i * own, (i + 1) * own)
            part = jnp.dot(dhi[rows, :], w[...], preferred_element_type=F32)
            part += jnp.dot(dlo[rows, :], w[...], preferred_element_type=F32)
            part = part + pltpu.roll(part, half, 1)
            piece[i] = jnp.where(low_lanes((bit, 2 * half), half), part[:bit], part[bit:])
            e_copy(i).start()

    @pl.when(diag)
    def _():
        for i in range(n):
            top = both[i * own:i * own + bit, :]
            bottom = both[i * own + bit:(i + 1) * own, :]
            value = jnp.where(low_lanes((bit, 2 * half), half), top, bottom)
            piece[i] = value

            @pl.when((i != r) if i >= early else ((i != r) & (r < n - 1)))
            def _():
                s_copy(i).start()

            @pl.when(i == r)
            def _():
                place(value)

    @pl.when(jnp.logical_not(diag))
    def _():
        s_copy(0).wait_recv()
        place(pin_slice[...])

    @pl.when(lower)
    def _():
        for m in range(chunks):
            p_copy(m).wait_send()

    for i in range(n):
        @pl.when(diag & (i > r))
        def _():
            for m in range(chunks):
                x_copy(i, m).wait_send()

        @pl.when(diag & ((i != r) if i >= early else ((i != r) & (r < n - 1))))
        def _():
            s_copy(i).wait_send()

    @pl.when((r == n - 1) & (c < n - 2))
    def _():
        for m in range(chunks):
            h_copy(m).wait_send()

    @pl.when(final)
    def _():
        for q in range(2):
            d_copy(q).wait_send()

    @pl.when(helper)
    def _():
        for i in range(early):
            e_copy(i).wait_send()


def local(n, factor, rhs, pattern):
    size, columns = rhs.shape[1], rhs.shape[2]
    step = 256 if size % 256 == 0 else size
    chunks = size // step
    half = columns
    own = size // n
    dma = pltpu.SemaphoreType.DMA
    solved = pl.pallas_call(
        functools.partial(kernel, n, size, step, half),
        out_shape=jax.ShapeDtypeStruct((1, columns, own), F32),
        in_specs=[
            pl.BlockSpec(memory_space=pltpu.HBM),
            pl.BlockSpec(memory_space=pltpu.HBM),
            pl.BlockSpec(memory_space=pltpu.HBM),
        ],
        out_specs=pl.BlockSpec(memory_space=pltpu.VMEM),
        scratch_shapes=[
            pltpu.SMEM(pattern.shape, jnp.int32),
            pltpu.VMEM((size, size), F32),
            pltpu.VMEM((size, size), BF),
            pltpu.VMEM((size, size), BF),
            pltpu.VMEM((columns, size), F32),
            pltpu.VMEM((size, 2 * half), BF),
            pltpu.VMEM((size, 2 * half), F32),
            pltpu.VMEM((size, 2 * half), F32),
            pltpu.VMEM((chunks, step // 2, 2 * half), F32),
            pltpu.VMEM((chunks, step // 2, 2 * half), F32),
            pltpu.VMEM((n - 1, chunks, step // 2, 2 * half), F32),
            pltpu.VMEM((n, own // 2, 2 * half), F32),
            pltpu.VMEM((own // 2, 2 * half), F32),
            pltpu.VMEM((n // 2 * own, size), F32),
            pltpu.VMEM((n // 2 * own, size), BF),
            pltpu.VMEM((n // 2 * own, size), BF),
            dma((chunks,)),
            dma,
            dma,
            dma((n, chunks)),
            dma((chunks,)),
            dma((chunks,)),
            dma((n - 1, chunks)),
            dma((n,)),
            dma,
            dma((2,)),
            dma((2,)),
            dma((chunks,)),
        ],
        compiler_params=pltpu.CompilerParams(
            collective_id=0, has_side_effects=True, vmem_limit_bytes=40 * 1024 * 1024
        ),
    )(*[pltpu.with_memory_space_constraint(v, pltpu.HBM) for v in (factor, jnp.swapaxes(rhs, 1, 2), pattern)])
    return jnp.swapaxes(solved, 1, 2)


def solution(mesh):
    in_specs = (P(("grp", "row"), "col", None, None), P(("grp", "row"), None, None), P("grp", None))
    out_specs = P(("grp", "col"), "row", None)
    return jax.shard_map(
        functools.partial(local, mesh.shape["row"]),
        mesh=mesh, in_specs=in_specs, out_specs=out_specs, check_vma=False,
    )
```

```python
import functools

import jax
import jax.numpy as jnp
from jax import lax
from jax.experimental import pallas as pl
from jax.experimental.pallas import tpu as pltpu
from jax.sharding import PartitionSpec as P

MESH = pl.DeviceIdType.MESH
BF = jnp.bfloat16
F32 = jnp.float32


def low_lanes(shape, half):
    return lax.broadcasted_iota(jnp.int32, shape, 1) < half


def halves(packed, half):
    low = low_lanes(packed.shape, half)
    lead = packed.astype(BF).astype(F32)
    rest = packed - lead
    upper = jnp.where(low, lead, pltpu.roll(rest, half, 1))
    lower = jnp.where(low, pltpu.roll(lead, half, 1), rest)
    return upper.astype(BF), lower.astype(BF)


def kernel(
    n, size, step, half,
    factor, rhs, pattern, out,
    links, a32, ahi, alo, right, w, acc, both, sent, xin, pin, piece, pin_slice, d32, dhi, dlo,
    a_sem, r_sem, l_sem, x_send, x_recv, p_send, p_recv, s_send, s_recv, d_send, d_recv,
):
    r = lax.axis_index("row")
    c = lax.axis_index("col")
    chunks = size // step
    mid = step // 2
    own = size // n
    bit = own // 2
    diag = r == c
    lower = r > c
    active = r >= c
    helper = (r == n - 1) & (c == n - 2)
    final = (r == n - 1) & (c == n - 1)
    early = n // 2
    from_helper = (c == n - 1) & (r < early)

    def load(k):
        rows = pl.ds(k * step, step)
        return pltpu.make_async_copy(factor.at[0, 0, rows, :], a32.at[rows, :], a_sem.at[k])

    def load_right():
        return pltpu.make_async_copy(rhs.at[0], right, r_sem)

    def load_links():
        return pltpu.make_async_copy(pattern, links, l_sem)

    @pl.when(active)
    def _():
        load_links().start()

    @pl.when(diag | helper)
    def _():
        load_right().start()

    @pl.when(active)
    def _():
        for k in range(chunks):
            load(k).start()

    barrier = pltpu.get_barrier_semaphore()
    for i in range(n):
        @pl.when(diag & (i < r) & ((r < n - 1) | (i == n - 2)))
        def _():
            pl.semaphore_signal(barrier, inc=1, device_id={"col": i}, device_id_type=MESH)

    @pl.when(jnp.logical_not(diag) & jnp.logical_not(from_helper))
    def _():
        pl.semaphore_signal(barrier, inc=1, device_id={"row": c}, device_id_type=MESH)

    @pl.when(from_helper)
    def _():
        pl.semaphore_signal(
            barrier, inc=1, device_id={"row": n - 1, "col": n - 2}, device_id_type=MESH
        )

    @pl.when(helper)
    def _():
        for j in range(n):
            if j != n - 2:
                pl.semaphore_signal(barrier, inc=1, device_id={"col": j}, device_id_type=MESH)

    block = 64
    part_rows = early * own // 2

    def prepare(k, keep):
        load(k).wait()

        def split(t, carry):
            rows = pl.ds(pl.multiple_of(k * step + t * block, block), block)
            full = a32[rows, :] * keep
            lead = full.astype(BF)
            ahi[rows, :] = lead
            alo[rows, :] = (full - lead.astype(F32)).astype(BF)
            return carry

        lax.fori_loop(0, step // block, split, 0)

    def x_copy(i, m):
        return pltpu.make_async_remote_copy(
            src_ref=sent.at[m], dst_ref=xin.at[m], send_sem=x_send.at[i, m], recv_sem=x_recv.at[m],
            device_id={"row": i}, device_id_type=MESH,
        )

    def p_copy(m):
        return pltpu.make_async_remote_copy(
            src_ref=sent.at[m], dst_ref=pin.at[c, m], send_sem=p_send.at[m], recv_sem=p_recv.at[c, m],
            device_id={"col": jnp.where((r == n - 1) & (c < n - 2), n - 2, r)}, device_id_type=MESH,
        )

    def p_arrival(j, m):
        return pltpu.make_async_remote_copy(
            src_ref=sent.at[m], dst_ref=pin.at[j, m], send_sem=p_send.at[m], recv_sem=p_recv.at[j, m],
            device_id={"col": r}, device_id_type=MESH,
        )

    def d_copy(q):
        rows = pl.ds(q * part_rows, part_rows)
        return pltpu.make_async_remote_copy(
            src_ref=factor.at[0, 0, rows, :], dst_ref=d32.at[rows, :],
            send_sem=d_send.at[q], recv_sem=d_recv.at[q],
            device_id={"col": n - 2}, device_id_type=MESH,
        )

    def e_copy(i):
        return pltpu.make_async_remote_copy(
            src_ref=piece.at[i], dst_ref=pin_slice, send_sem=s_send.at[i], recv_sem=s_recv,
            device_id={"row": i, "col": n - 1}, device_id_type=MESH,
        )

    def s_copy(i):
        return pltpu.make_async_remote_copy(
            src_ref=piece.at[i], dst_ref=pin_slice, send_sem=s_send.at[i], recv_sem=s_recv,
            device_id={"row": i}, device_id_type=MESH,
        )

    def place(value):
        turned = value.T
        out[0, :, :bit] = turned[:half]
        out[0, :, bit:] = turned[half:]

    def weave(k, value):
        first, second = halves(value, half)
        w[k * step:k * step + mid, :] = first
        w[k * step + mid:(k + 1) * step, :] = second

    def product(rows, cols):
        part = jnp.dot(ahi[rows, cols], w[cols, :], preferred_element_type=F32)
        return part + jnp.dot(alo[rows, cols], w[cols, :], preferred_element_type=F32)

    def finish(m, part):
        part = part + pltpu.roll(part, half, 1)
        both[m * step:(m + 1) * step, :] = part
        sent[m] = jnp.where(low_lanes((mid, 2 * half), half), part[:mid], part[mid:])

    def right_chunk(k):
        base = k * step
        return jnp.concatenate(
            [right[:, base:base + mid], right[:, base + mid:base + step]], axis=0
        ).T

    @pl.when(diag | helper)
    def _():
        load_right().wait()

    @pl.when(diag)
    def _():
        for k in range(chunks):
            xin[k] = right_chunk(k)

    @pl.when(active)
    def _():
        load_links().wait()

    @pl.when(diag & (r == 0))
    def _():
        for k in range(chunks):
            weave(k, xin[k])
        for m in range(chunks):
            prepare(m, jnp.float32(1.0))
            finish(m, product(slice(m * step, (m + 1) * step), slice(0, size)))
            if m == 0:
                pl.semaphore_wait(barrier, n - 1)
            x_copy(1, m).start()

    @pl.when(active & (r > 0))
    def _():
        keep = jnp.where(diag | (links[r, c] == 1), 1.0, 0.0).astype(F32)

        @pl.when(final)
        def _():
            pl.semaphore_wait(barrier, n - early)
            for q in range(2):
                d_copy(q).start()

        for k in range(chunks):
            prepare(k, keep)

        @pl.when(diag & (r < n - 1))
        def _():
            pl.semaphore_wait(barrier, n - 1)

        @pl.when(lower & jnp.logical_not(helper))
        def _():
            pl.semaphore_wait(barrier, 1)

        @pl.when(helper)
        def _():
            pl.semaphore_wait(barrier, 1 + early)
            for q in range(2):
                d_copy(q).wait_recv()
            strip = 16

            def split(t, carry):
                rows = pl.ds(pl.multiple_of(t * strip, strip), strip)
                full = d32[rows, :]
                lead = full.astype(BF)
                dhi[rows, :] = lead
                dlo[rows, :] = (full - lead.astype(F32)).astype(BF)
                return carry

            lax.fori_loop(0, early * own // strip, split, 0)

        for k in range(chunks):
            base = k * step

            @pl.when(lower)
            def _():
                x_copy(0, k).wait_recv()

            for j in range(n - 2):
                @pl.when(diag & (j < r) & (r < n - 1))
                def _():
                    p_arrival(j, k).wait_recv()
                    xin[k] = xin[k] - pin[j, k]

            @pl.when(final)
            def _():
                p_arrival(n - 2, k).wait_recv()
                xin[k] = pin[n - 2, k]

            weave(k, xin[k])
            last = k == chunks - 1
            for m in range(chunks):
                rows = slice(m * step, (m + 1) * step)
                part = product(rows, slice(base, base + step))
                if k:
                    part += acc[rows, :]
                if not last:
                    acc[rows, :] = part
                    continue
                finish(m, part)

                @pl.when(helper)
                def _():
                    value = right_chunk(m) - sent[m]
                    for j in range(n - 2):
                        p_arrival(j, m).wait_recv()
                        value = value - pin[j, m]
                    sent[m] = value

                @pl.when(lower)
                def _():
                    p_copy(m).start()

                for i in range(2, n):
                    @pl.when(diag & (i == r + 1))
                    def _():
                        x_copy(i, m).start()

    for i in range(2, n):
        @pl.when(diag & (i > r + 1))
        def _():
            for m in range(chunks):
                x_copy(i, m).start()

    @pl.when(helper)
    def _():
        for k in range(chunks):
            weave(k, sent[k])
        for i in range(early):
            rows = slice(i * own, (i + 1) * own)
            part = jnp.dot(dhi[rows, :], w[...], preferred_element_type=F32)
            part += jnp.dot(dlo[rows, :], w[...], preferred_element_type=F32)
            part = part + pltpu.roll(part, half, 1)
            piece[i] = jnp.where(low_lanes((bit, 2 * half), half), part[:bit], part[bit:])
            e_copy(i).start()

    @pl.when(diag)
    def _():
        for i in range(n):
            top = both[i * own:i * own + bit, :]
            bottom = both[i * own + bit:(i + 1) * own, :]
            value = jnp.where(low_lanes((bit, 2 * half), half), top, bottom)
            piece[i] = value

            @pl.when((i != r) if i >= early else ((i != r) & (r < n - 1)))
            def _():
                s_copy(i).start()

            @pl.when(i == r)
            def _():
                place(value)

    @pl.when(jnp.logical_not(diag))
    def _():
        s_copy(0).wait_recv()
        place(pin_slice[...])

    @pl.when(lower)
    def _():
        for m in range(chunks):
            p_copy(m).wait_send()

    for i in range(n):
        @pl.when(diag & (i > r))
        def _():
            for m in range(chunks):
                x_copy(i, m).wait_send()

        @pl.when(diag & ((i != r) if i >= early else ((i != r) & (r < n - 1))))
        def _():
            s_copy(i).wait_send()

    @pl.when(final)
    def _():
        for q in range(2):
            d_copy(q).wait_send()

    @pl.when(helper)
    def _():
        for i in range(early):
            e_copy(i).wait_send()


def local(n, factor, rhs, pattern):
    size, columns = rhs.shape[1], rhs.shape[2]
    step = 256 if size % 256 == 0 else size
    chunks = size // step
    half = columns
    own = size // n
    dma = pltpu.SemaphoreType.DMA
    solved = pl.pallas_call(
        functools.partial(kernel, n, size, step, half),
        out_shape=jax.ShapeDtypeStruct((1, columns, own), F32),
        in_specs=[
            pl.BlockSpec(memory_space=pltpu.HBM),
            pl.BlockSpec(memory_space=pltpu.HBM),
            pl.BlockSpec(memory_space=pltpu.HBM),
        ],
        out_specs=pl.BlockSpec(memory_space=pltpu.VMEM),
        scratch_shapes=[
            pltpu.SMEM(pattern.shape, jnp.int32),
            pltpu.VMEM((size, size), F32),
            pltpu.VMEM((size, size), BF),
            pltpu.VMEM((size, size), BF),
            pltpu.VMEM((columns, size), F32),
            pltpu.VMEM((size, 2 * half), BF),
            pltpu.VMEM((size, 2 * half), F32),
            pltpu.VMEM((size, 2 * half), F32),
            pltpu.VMEM((chunks, step // 2, 2 * half), F32),
            pltpu.VMEM((chunks, step // 2, 2 * half), F32),
            pltpu.VMEM((n - 1, chunks, step // 2, 2 * half), F32),
            pltpu.VMEM((n, own // 2, 2 * half), F32),
            pltpu.VMEM((own // 2, 2 * half), F32),
            pltpu.VMEM((n // 2 * own, size), F32),
            pltpu.VMEM((n // 2 * own, size), BF),
            pltpu.VMEM((n // 2 * own, size), BF),
            dma((chunks,)),
            dma,
            dma,
            dma((n, chunks)),
            dma((chunks,)),
            dma((chunks,)),
            dma((n - 1, chunks)),
            dma((n,)),
            dma,
            dma((2,)),
            dma((2,)),
        ],
        compiler_params=pltpu.CompilerParams(
            collective_id=0, has_side_effects=True, vmem_limit_bytes=40 * 1024 * 1024
        ),
    )(*[pltpu.with_memory_space_constraint(v, pltpu.HBM) for v in (factor, jnp.swapaxes(rhs, 1, 2), pattern)])
    return jnp.swapaxes(solved, 1, 2)


def solution(mesh):
    in_specs = (P(("grp", "row"), "col", None, None), P(("grp", "row"), None, None), P("grp", None))
    out_specs = P(("grp", "col"), "row", None)
    return jax.shard_map(
        functools.partial(local, mesh.shape["row"]),
        mesh=mesh, in_specs=in_specs, out_specs=out_specs, check_vma=False,
    )
```

```python
import functools

import jax
import jax.numpy as jnp
from jax import lax
from jax.experimental import pallas as pl
from jax.experimental.pallas import tpu as pltpu
from jax.sharding import PartitionSpec as P

MESH = pl.DeviceIdType.MESH
BF = jnp.bfloat16
F32 = jnp.float32


def low_lanes(shape, half):
    return lax.broadcasted_iota(jnp.int32, shape, 1) < half


def halves(packed, half):
    low = low_lanes(packed.shape, half)
    lead = packed.astype(BF).astype(F32)
    rest = packed - lead
    upper = jnp.where(low, lead, pltpu.roll(rest, half, 1))
    lower = jnp.where(low, pltpu.roll(lead, half, 1), rest)
    return upper.astype(BF), lower.astype(BF)


def kernel(
    n, size, step, half,
    factor, rhs, pattern, out,
    links, a32, ahi, alo, right, w, acc, both, sent, xin, pin, piece, pin_slice, d32, dhi, dlo,
    a_sem, r_sem, l_sem, x_send, x_recv, p_send, p_recv, s_send, s_recv, d_send, d_recv, f_send,
):
    r = lax.axis_index("row")
    c = lax.axis_index("col")
    chunks = size // step
    mid = step // 2
    own = size // n
    bit = own // 2
    diag = r == c
    lower = r > c
    active = r >= c
    helper = (r == n - 1) & (c == n - 2)
    final = (r == n - 1) & (c == n - 1)
    early = n // 2
    from_helper = (c == n - 1) & (r < early)
    passes = lower & (lax.rem(r, 2) == 0) & (r < n - 1)
    passed = (lax.rem(r, 2) == 1) & (r - 1 > c)

    def load(k):
        rows = pl.ds(k * step, step)
        return pltpu.make_async_copy(factor.at[0, 0, rows, :], a32.at[rows, :], a_sem.at[k])

    def load_right():
        return pltpu.make_async_copy(rhs.at[0], right, r_sem)

    def load_links():
        return pltpu.make_async_copy(pattern, links, l_sem)

    @pl.when(active)
    def _():
        load_links().start()

    @pl.when(diag | helper)
    def _():
        load_right().start()

    @pl.when(active)
    def _():
        for k in range(chunks):
            load(k).start()

    barrier = pltpu.get_barrier_semaphore()
    for i in range(n):
        @pl.when(diag & (i < r) & ((r < n - 1) | (i == n - 2)))
        def _():
            pl.semaphore_signal(barrier, inc=1, device_id={"col": i}, device_id_type=MESH)

    @pl.when(jnp.logical_not(diag) & jnp.logical_not(from_helper))
    def _():
        pl.semaphore_signal(barrier, inc=1, device_id={"row": c}, device_id_type=MESH)

    @pl.when(passed)
    def _():
        pl.semaphore_signal(barrier, inc=1, device_id={"row": r - 1}, device_id_type=MESH)

    @pl.when(from_helper)
    def _():
        pl.semaphore_signal(
            barrier, inc=1, device_id={"row": n - 1, "col": n - 2}, device_id_type=MESH
        )

    @pl.when(helper)
    def _():
        for j in range(n):
            if j != n - 2:
                pl.semaphore_signal(barrier, inc=1, device_id={"col": j}, device_id_type=MESH)

    block = 64
    part_rows = early * own // 2

    def prepare(k, keep):
        load(k).wait()

        def split(t, carry):
            rows = pl.ds(pl.multiple_of(k * step + t * block, block), block)
            full = a32[rows, :] * keep
            lead = full.astype(BF)
            ahi[rows, :] = lead
            alo[rows, :] = (full - lead.astype(F32)).astype(BF)
            return carry

        lax.fori_loop(0, step // block, split, 0)

    def x_copy(i, m):
        return pltpu.make_async_remote_copy(
            src_ref=sent.at[m], dst_ref=xin.at[m], send_sem=x_send.at[i, m], recv_sem=x_recv.at[m],
            device_id={"row": i}, device_id_type=MESH,
        )

    def p_copy(m):
        return pltpu.make_async_remote_copy(
            src_ref=sent.at[m], dst_ref=pin.at[c, m], send_sem=p_send.at[m], recv_sem=p_recv.at[c, m],
            device_id={"col": jnp.where((r == n - 1) & (c < n - 2), n - 2, r)}, device_id_type=MESH,
        )

    def p_arrival(j, m):
        return pltpu.make_async_remote_copy(
            src_ref=sent.at[m], dst_ref=pin.at[j, m], send_sem=p_send.at[m], recv_sem=p_recv.at[j, m],
            device_id={"col": r}, device_id_type=MESH,
        )

    def f_copy(m):
        return pltpu.make_async_remote_copy(
            src_ref=xin.at[m], dst_ref=xin.at[m], send_sem=f_send.at[m], recv_sem=x_recv.at[m],
            device_id={"row": r + 1}, device_id_type=MESH,
        )

    def d_copy(q):
        rows = pl.ds(q * part_rows, part_rows)
        return pltpu.make_async_remote_copy(
            src_ref=factor.at[0, 0, rows, :], dst_ref=d32.at[rows, :],
            send_sem=d_send.at[q], recv_sem=d_recv.at[q],
            device_id={"col": n - 2}, device_id_type=MESH,
        )

    def e_copy(i):
        return pltpu.make_async_remote_copy(
            src_ref=piece.at[i], dst_ref=pin_slice, send_sem=s_send.at[i], recv_sem=s_recv,
            device_id={"row": i, "col": n - 1}, device_id_type=MESH,
        )

    def s_copy(i):
        return pltpu.make_async_remote_copy(
            src_ref=piece.at[i], dst_ref=pin_slice, send_sem=s_send.at[i], recv_sem=s_recv,
            device_id={"row": i}, device_id_type=MESH,
        )

    def place(value):
        turned = value.T
        out[0, :, :bit] = turned[:half]
        out[0, :, bit:] = turned[half:]

    def weave(k, value):
        first, second = halves(value, half)
        w[k * step:k * step + mid, :] = first
        w[k * step + mid:(k + 1) * step, :] = second

    def product(rows, cols):
        part = jnp.dot(ahi[rows, cols], w[cols, :], preferred_element_type=F32)
        return part + jnp.dot(alo[rows, cols], w[cols, :], preferred_element_type=F32)

    def finish(m, part):
        part = part + pltpu.roll(part, half, 1)
        both[m * step:(m + 1) * step, :] = part
        sent[m] = jnp.where(low_lanes((mid, 2 * half), half), part[:mid], part[mid:])

    def right_chunk(k):
        base = k * step
        return jnp.concatenate(
            [right[:, base:base + mid], right[:, base + mid:base + step]], axis=0
        ).T

    @pl.when(diag | helper)
    def _():
        load_right().wait()

    @pl.when(diag)
    def _():
        for k in range(chunks):
            xin[k] = right_chunk(k)

    @pl.when(active)
    def _():
        load_links().wait()

    @pl.when(diag & (r == 0))
    def _():
        for k in range(chunks):
            weave(k, xin[k])
        for m in range(chunks):
            prepare(m, jnp.float32(1.0))
            finish(m, product(slice(m * step, (m + 1) * step), slice(0, size)))
            if m == 0:
                pl.semaphore_wait(barrier, n - 1)
            x_copy(1, m).start()

    @pl.when(active & (r > 0))
    def _():
        keep = jnp.where(diag | (links[r, c] == 1), 1.0, 0.0).astype(F32)

        @pl.when(final)
        def _():
            pl.semaphore_wait(barrier, n - early)
            for q in range(2):
                d_copy(q).start()

        for k in range(chunks):
            prepare(k, keep)

        @pl.when(diag & (r < n - 1))
        def _():
            pl.semaphore_wait(barrier, n - 1)

        @pl.when(lower & jnp.logical_not(helper) & jnp.logical_not(passes))
        def _():
            pl.semaphore_wait(barrier, 1)

        @pl.when(passes)
        def _():
            pl.semaphore_wait(barrier, 2)

        @pl.when(helper)
        def _():
            pl.semaphore_wait(barrier, 1 + early)
            for q in range(2):
                d_copy(q).wait_recv()
            strip = 16

            def split(t, carry):
                rows = pl.ds(pl.multiple_of(t * strip, strip), strip)
                full = d32[rows, :]
                lead = full.astype(BF)
                dhi[rows, :] = lead
                dlo[rows, :] = (full - lead.astype(F32)).astype(BF)
                return carry

            lax.fori_loop(0, early * own // strip, split, 0)

        for k in range(chunks):
            base = k * step

            @pl.when(lower)
            def _():
                x_copy(0, k).wait_recv()

            for j in range(n - 2):
                @pl.when(diag & (j < r) & (r < n - 1))
                def _():
                    p_arrival(j, k).wait_recv()
                    xin[k] = xin[k] - pin[j, k]

            @pl.when(final)
            def _():
                p_arrival(n - 2, k).wait_recv()
                xin[k] = pin[n - 2, k]

            weave(k, xin[k])
            last = k == chunks - 1
            for m in range(chunks):
                rows = slice(m * step, (m + 1) * step)
                part = product(rows, slice(base, base + step))
                if k:
                    part += acc[rows, :]
                if not last:
                    acc[rows, :] = part
                    continue
                finish(m, part)

                @pl.when(helper)
                def _():
                    value = right_chunk(m) - sent[m]
                    for j in range(n - 2):
                        p_arrival(j, m).wait_recv()
                        value = value - pin[j, m]
                    sent[m] = value

                @pl.when(lower)
                def _():
                    p_copy(m).start()

                for i in range(2, n):
                    @pl.when(diag & (i == r + 1))
                    def _():
                        x_copy(i, m).start()

    @pl.when(passes)
    def _():
        for m in range(chunks):
            f_copy(m).start()

    for i in range(1, n):
        @pl.when(diag & (i == r + 1))
        def _():
            for m in range(chunks):
                x_copy(i, m).wait_send()

    for i in range(2, n, 2):
        @pl.when(diag & (i > r + 1))
        def _():
            for m in range(chunks):
                x_copy(i, m).start()

    @pl.when(helper)
    def _():
        for k in range(chunks):
            weave(k, sent[k])
        for i in range(early):
            rows = slice(i * own, (i + 1) * own)
            part = jnp.dot(dhi[rows, :], w[...], preferred_element_type=F32)
            part += jnp.dot(dlo[rows, :], w[...], preferred_element_type=F32)
            part = part + pltpu.roll(part, half, 1)
            piece[i] = jnp.where(low_lanes((bit, 2 * half), half), part[:bit], part[bit:])
            e_copy(i).start()

    @pl.when(diag)
    def _():
        for i in range(n):
            top = both[i * own:i * own + bit, :]
            bottom = both[i * own + bit:(i + 1) * own, :]
            value = jnp.where(low_lanes((bit, 2 * half), half), top, bottom)
            piece[i] = value

            @pl.when((i != r) if i >= early else ((i != r) & (r < n - 1)))
            def _():
                s_copy(i).start()

            @pl.when(i == r)
            def _():
                place(value)

    @pl.when(jnp.logical_not(diag))
    def _():
        s_copy(0).wait_recv()
        place(pin_slice[...])

    @pl.when(lower)
    def _():
        for m in range(chunks):
            p_copy(m).wait_send()

    for i in range(n):
        if i % 2 == 0:
            @pl.when(diag & (i > r + 1))
            def _():
                for m in range(chunks):
                    x_copy(i, m).wait_send()

        @pl.when(diag & ((i != r) if i >= early else ((i != r) & (r < n - 1))))
        def _():
            s_copy(i).wait_send()

    @pl.when(passes)
    def _():
        for m in range(chunks):
            f_copy(m).wait_send()

    @pl.when(final)
    def _():
        for q in range(2):
            d_copy(q).wait_send()

    @pl.when(helper)
    def _():
        for i in range(early):
            e_copy(i).wait_send()


def local(n, factor, rhs, pattern):
    size, columns = rhs.shape[1], rhs.shape[2]
    step = 256 if size % 256 == 0 else size
    chunks = size // step
    half = columns
    own = size // n
    dma = pltpu.SemaphoreType.DMA
    solved = pl.pallas_call(
        functools.partial(kernel, n, size, step, half),
        out_shape=jax.ShapeDtypeStruct((1, columns, own), F32),
        in_specs=[
            pl.BlockSpec(memory_space=pltpu.HBM),
            pl.BlockSpec(memory_space=pltpu.HBM),
            pl.BlockSpec(memory_space=pltpu.HBM),
        ],
        out_specs=pl.BlockSpec(memory_space=pltpu.VMEM),
        scratch_shapes=[
            pltpu.SMEM(pattern.shape, jnp.int32),
            pltpu.VMEM((size, size), F32),
            pltpu.VMEM((size, size), BF),
            pltpu.VMEM((size, size), BF),
            pltpu.VMEM((columns, size), F32),
            pltpu.VMEM((size, 2 * half), BF),
            pltpu.VMEM((size, 2 * half), F32),
            pltpu.VMEM((size, 2 * half), F32),
            pltpu.VMEM((chunks, step // 2, 2 * half), F32),
            pltpu.VMEM((chunks, step // 2, 2 * half), F32),
            pltpu.VMEM((n - 1, chunks, step // 2, 2 * half), F32),
            pltpu.VMEM((n, own // 2, 2 * half), F32),
            pltpu.VMEM((own // 2, 2 * half), F32),
            pltpu.VMEM((n // 2 * own, size), F32),
            pltpu.VMEM((n // 2 * own, size), BF),
            pltpu.VMEM((n // 2 * own, size), BF),
            dma((chunks,)),
            dma,
            dma,
            dma((n, chunks)),
            dma((chunks,)),
            dma((chunks,)),
            dma((n - 1, chunks)),
            dma((n,)),
            dma,
            dma((2,)),
            dma((2,)),
            dma((chunks,)),
        ],
        compiler_params=pltpu.CompilerParams(
            collective_id=0, has_side_effects=True, vmem_limit_bytes=40 * 1024 * 1024
        ),
    )(*[pltpu.with_memory_space_constraint(v, pltpu.HBM) for v in (factor, jnp.swapaxes(rhs, 1, 2), pattern)])
    return jnp.swapaxes(solved, 1, 2)


def solution(mesh):
    in_specs = (P(("grp", "row"), "col", None, None), P(("grp", "row"), None, None), P("grp", None))
    out_specs = P(("grp", "col"), "row", None)
    return jax.shard_map(
        functools.partial(local, mesh.shape["row"]),
        mesh=mesh, in_specs=in_specs, out_specs=out_specs, check_vma=False,
    )
```

```python
import functools

import jax
import jax.numpy as jnp
from jax import lax
from jax.experimental import pallas as pl
from jax.experimental.pallas import tpu as pltpu
from jax.sharding import PartitionSpec as P

MESH = pl.DeviceIdType.MESH
BF = jnp.bfloat16
F32 = jnp.float32


def low_lanes(shape, half):
    return lax.broadcasted_iota(jnp.int32, shape, 1) < half


def halves(packed, half):
    low = low_lanes(packed.shape, half)
    lead = packed.astype(BF).astype(F32)
    rest = packed - lead
    upper = jnp.where(low, lead, pltpu.roll(rest, half, 1))
    lower = jnp.where(low, pltpu.roll(lead, half, 1), rest)
    return upper.astype(BF), lower.astype(BF)


def kernel(
    n, size, step, half,
    factor, rhs, pattern, out,
    links, a32, ahi, alo, right, w, acc, both, sent, xin, pin, piece, pin_slice, d32, dhi, dlo,
    a_sem, r_sem, l_sem, x_send, x_recv, p_send, p_recv, s_send, s_recv, d_send, d_recv, f_send,
):
    r = lax.axis_index("row")
    c = lax.axis_index("col")
    chunks = size // step
    mid = step // 2
    own = size // n
    bit = own // 2
    diag = r == c
    lower = r > c
    active = r >= c
    helper = (r == n - 1) & (c == n - 2)
    final = (r == n - 1) & (c == n - 1)
    early = n // 2
    from_helper = (c == n - 1) & (r < early)
    passes = lower & (lax.rem(r, 2) == 0) & (r < n - 1) & (c > 0)
    passed = (lax.rem(r, 2) == 1) & (r - 1 > c) & (c > 0)

    def load(k):
        rows = pl.ds(k * step, step)
        return pltpu.make_async_copy(factor.at[0, 0, rows, :], a32.at[rows, :], a_sem.at[k])

    def load_right():
        return pltpu.make_async_copy(rhs.at[0], right, r_sem)

    def load_links():
        return pltpu.make_async_copy(pattern, links, l_sem)

    @pl.when(active)
    def _():
        load_links().start()

    @pl.when(diag | helper)
    def _():
        load_right().start()

    @pl.when(active)
    def _():
        for k in range(chunks):
            load(k).start()

    barrier = pltpu.get_barrier_semaphore()
    for i in range(n):
        @pl.when(diag & (i < r) & ((r < n - 1) | (i == n - 2)))
        def _():
            pl.semaphore_signal(barrier, inc=1, device_id={"col": i}, device_id_type=MESH)

    @pl.when(jnp.logical_not(diag) & jnp.logical_not(from_helper))
    def _():
        pl.semaphore_signal(barrier, inc=1, device_id={"row": c}, device_id_type=MESH)

    @pl.when(passed)
    def _():
        pl.semaphore_signal(barrier, inc=1, device_id={"row": r - 1}, device_id_type=MESH)

    @pl.when(from_helper)
    def _():
        pl.semaphore_signal(
            barrier, inc=1, device_id={"row": n - 1, "col": n - 2}, device_id_type=MESH
        )

    @pl.when(helper)
    def _():
        for j in range(n):
            if j != n - 2:
                pl.semaphore_signal(barrier, inc=1, device_id={"col": j}, device_id_type=MESH)

    block = 64
    part_rows = early * own // 2

    def prepare(k, keep):
        load(k).wait()

        def split(t, carry):
            rows = pl.ds(pl.multiple_of(k * step + t * block, block), block)
            full = a32[rows, :] * keep
            lead = full.astype(BF)
            ahi[rows, :] = lead
            alo[rows, :] = (full - lead.astype(F32)).astype(BF)
            return carry

        lax.fori_loop(0, step // block, split, 0)

    def x_copy(i, m):
        return pltpu.make_async_remote_copy(
            src_ref=sent.at[m], dst_ref=xin.at[m], send_sem=x_send.at[i, m], recv_sem=x_recv.at[m],
            device_id={"row": i}, device_id_type=MESH,
        )

    def p_copy(m):
        return pltpu.make_async_remote_copy(
            src_ref=sent.at[m], dst_ref=pin.at[c, m], send_sem=p_send.at[m], recv_sem=p_recv.at[c, m],
            device_id={"col": jnp.where((r == n - 1) & (c < n - 2), n - 2, r)}, device_id_type=MESH,
        )

    def p_arrival(j, m):
        return pltpu.make_async_remote_copy(
            src_ref=sent.at[m], dst_ref=pin.at[j, m], send_sem=p_send.at[m], recv_sem=p_recv.at[j, m],
            device_id={"col": r}, device_id_type=MESH,
        )

    def f_copy(m):
        return pltpu.make_async_remote_copy(
            src_ref=xin.at[m], dst_ref=xin.at[m], send_sem=f_send.at[m], recv_sem=x_recv.at[m],
            device_id={"row": r + 1}, device_id_type=MESH,
        )

    def d_copy(q):
        rows = pl.ds(q * part_rows, part_rows)
        return pltpu.make_async_remote_copy(
            src_ref=factor.at[0, 0, rows, :], dst_ref=d32.at[rows, :],
            send_sem=d_send.at[q], recv_sem=d_recv.at[q],
            device_id={"col": n - 2}, device_id_type=MESH,
        )

    def e_copy(i):
        return pltpu.make_async_remote_copy(
            src_ref=piece.at[i], dst_ref=pin_slice, send_sem=s_send.at[i], recv_sem=s_recv,
            device_id={"row": i, "col": n - 1}, device_id_type=MESH,
        )

    def s_copy(i):
        return pltpu.make_async_remote_copy(
            src_ref=piece.at[i], dst_ref=pin_slice, send_sem=s_send.at[i], recv_sem=s_recv,
            device_id={"row": i}, device_id_type=MESH,
        )

    def place(value):
        turned = value.T
        out[0, :, :bit] = turned[:half]
        out[0, :, bit:] = turned[half:]

    def weave(k, value):
        first, second = halves(value, half)
        w[k * step:k * step + mid, :] = first
        w[k * step + mid:(k + 1) * step, :] = second

    def product(rows, cols):
        part = jnp.dot(ahi[rows, cols], w[cols, :], preferred_element_type=F32)
        return part + jnp.dot(alo[rows, cols], w[cols, :], preferred_element_type=F32)

    def finish(m, part):
        part = part + pltpu.roll(part, half, 1)
        both[m * step:(m + 1) * step, :] = part
        sent[m] = jnp.where(low_lanes((mid, 2 * half), half), part[:mid], part[mid:])

    def right_chunk(k):
        base = k * step
        return jnp.concatenate(
            [right[:, base:base + mid], right[:, base + mid:base + step]], axis=0
        ).T

    @pl.when(diag | helper)
    def _():
        load_right().wait()

    @pl.when(diag)
    def _():
        for k in range(chunks):
            xin[k] = right_chunk(k)

    @pl.when(active)
    def _():
        load_links().wait()

    @pl.when(diag & (r == 0))
    def _():
        for k in range(chunks):
            weave(k, xin[k])
        for m in range(chunks):
            prepare(m, jnp.float32(1.0))
            finish(m, product(slice(m * step, (m + 1) * step), slice(0, size)))
            if m == 0:
                pl.semaphore_wait(barrier, n - 1)
            x_copy(1, m).start()

    @pl.when(active & (r > 0))
    def _():
        keep = jnp.where(diag | (links[r, c] == 1), 1.0, 0.0).astype(F32)

        @pl.when(final)
        def _():
            pl.semaphore_wait(barrier, n - early)
            for q in range(2):
                d_copy(q).start()

        for k in range(chunks):
            prepare(k, keep)

        @pl.when(diag & (r < n - 1))
        def _():
            pl.semaphore_wait(barrier, n - 1)

        @pl.when(lower & jnp.logical_not(helper) & jnp.logical_not(passes))
        def _():
            pl.semaphore_wait(barrier, 1)

        @pl.when(passes)
        def _():
            pl.semaphore_wait(barrier, 2)

        @pl.when(helper)
        def _():
            pl.semaphore_wait(barrier, 1 + early)
            for q in range(2):
                d_copy(q).wait_recv()
            strip = 16

            def split(t, carry):
                rows = pl.ds(pl.multiple_of(t * strip, strip), strip)
                full = d32[rows, :]
                lead = full.astype(BF)
                dhi[rows, :] = lead
                dlo[rows, :] = (full - lead.astype(F32)).astype(BF)
                return carry

            lax.fori_loop(0, early * own // strip, split, 0)

        for k in range(chunks):
            base = k * step

            @pl.when(lower)
            def _():
                x_copy(0, k).wait_recv()

            for j in range(n - 2):
                @pl.when(diag & (j < r) & (r < n - 1))
                def _():
                    p_arrival(j, k).wait_recv()
                    xin[k] = xin[k] - pin[j, k]

            @pl.when(final)
            def _():
                p_arrival(n - 2, k).wait_recv()
                xin[k] = pin[n - 2, k]

            weave(k, xin[k])
            last = k == chunks - 1
            for m in range(chunks):
                rows = slice(m * step, (m + 1) * step)
                part = product(rows, slice(base, base + step))
                if k:
                    part += acc[rows, :]
                if not last:
                    acc[rows, :] = part
                    continue
                finish(m, part)

                @pl.when(helper)
                def _():
                    value = right_chunk(m) - sent[m]
                    for j in range(n - 2):
                        p_arrival(j, m).wait_recv()
                        value = value - pin[j, m]
                    sent[m] = value

                @pl.when(lower)
                def _():
                    p_copy(m).start()

                for i in range(2, n):
                    @pl.when(diag & (i == r + 1))
                    def _():
                        x_copy(i, m).start()

    @pl.when(passes)
    def _():
        for m in range(chunks):
            f_copy(m).start()

    for i in range(1, n):
        @pl.when(diag & (i == r + 1))
        def _():
            for m in range(chunks):
                x_copy(i, m).wait_send()

    for i in range(2, n):
        @pl.when(diag & (i > r + 1) & ((r == 0) | (i % 2 == 0)))
        def _():
            for m in range(chunks):
                x_copy(i, m).start()

    @pl.when(helper)
    def _():
        for k in range(chunks):
            weave(k, sent[k])
        for i in range(early):
            rows = slice(i * own, (i + 1) * own)
            part = jnp.dot(dhi[rows, :], w[...], preferred_element_type=F32)
            part += jnp.dot(dlo[rows, :], w[...], preferred_element_type=F32)
            part = part + pltpu.roll(part, half, 1)
            piece[i] = jnp.where(low_lanes((bit, 2 * half), half), part[:bit], part[bit:])
            e_copy(i).start()

    @pl.when(diag)
    def _():
        for i in range(n):
            top = both[i * own:i * own + bit, :]
            bottom = both[i * own + bit:(i + 1) * own, :]
            value = jnp.where(low_lanes((bit, 2 * half), half), top, bottom)
            piece[i] = value

            @pl.when((i != r) if i >= early else ((i != r) & (r < n - 1)))
            def _():
                s_copy(i).start()

            @pl.when(i == r)
            def _():
                place(value)

    @pl.when(jnp.logical_not(diag))
    def _():
        s_copy(0).wait_recv()
        place(pin_slice[...])

    @pl.when(lower)
    def _():
        for m in range(chunks):
            p_copy(m).wait_send()

    for i in range(n):
        @pl.when(diag & (i > r + 1) & ((r == 0) | (i % 2 == 0)))
        def _():
            for m in range(chunks):
                x_copy(i, m).wait_send()

        @pl.when(diag & ((i != r) if i >= early else ((i != r) & (r < n - 1))))
        def _():
            s_copy(i).wait_send()

    @pl.when(passes)
    def _():
        for m in range(chunks):
            f_copy(m).wait_send()

    @pl.when(final)
    def _():
        for q in range(2):
            d_copy(q).wait_send()

    @pl.when(helper)
    def _():
        for i in range(early):
            e_copy(i).wait_send()


def local(n, factor, rhs, pattern):
    size, columns = rhs.shape[1], rhs.shape[2]
    step = 256 if size % 256 == 0 else size
    chunks = size // step
    half = columns
    own = size // n
    dma = pltpu.SemaphoreType.DMA
    solved = pl.pallas_call(
        functools.partial(kernel, n, size, step, half),
        out_shape=jax.ShapeDtypeStruct((1, columns, own), F32),
        in_specs=[
            pl.BlockSpec(memory_space=pltpu.HBM),
            pl.BlockSpec(memory_space=pltpu.HBM),
            pl.BlockSpec(memory_space=pltpu.HBM),
        ],
        out_specs=pl.BlockSpec(memory_space=pltpu.VMEM),
        scratch_shapes=[
            pltpu.SMEM(pattern.shape, jnp.int32),
            pltpu.VMEM((size, size), F32),
            pltpu.VMEM((size, size), BF),
            pltpu.VMEM((size, size), BF),
            pltpu.VMEM((columns, size), F32),
            pltpu.VMEM((size, 2 * half), BF),
            pltpu.VMEM((size, 2 * half), F32),
            pltpu.VMEM((size, 2 * half), F32),
            pltpu.VMEM((chunks, step // 2, 2 * half), F32),
            pltpu.VMEM((chunks, step // 2, 2 * half), F32),
            pltpu.VMEM((n - 1, chunks, step // 2, 2 * half), F32),
            pltpu.VMEM((n, own // 2, 2 * half), F32),
            pltpu.VMEM((own // 2, 2 * half), F32),
            pltpu.VMEM((n // 2 * own, size), F32),
            pltpu.VMEM((n // 2 * own, size), BF),
            pltpu.VMEM((n // 2 * own, size), BF),
            dma((chunks,)),
            dma,
            dma,
            dma((n, chunks)),
            dma((chunks,)),
            dma((chunks,)),
            dma((n - 1, chunks)),
            dma((n,)),
            dma,
            dma((2,)),
            dma((2,)),
            dma((chunks,)),
        ],
        compiler_params=pltpu.CompilerParams(
            collective_id=0, has_side_effects=True, vmem_limit_bytes=40 * 1024 * 1024
        ),
    )(*[pltpu.with_memory_space_constraint(v, pltpu.HBM) for v in (factor, jnp.swapaxes(rhs, 1, 2), pattern)])
    return jnp.swapaxes(solved, 1, 2)


def solution(mesh):
    in_specs = (P(("grp", "row"), "col", None, None), P(("grp", "row"), None, None), P("grp", None))
    out_specs = P(("grp", "col"), "row", None)
    return jax.shard_map(
        functools.partial(local, mesh.shape["row"]),
        mesh=mesh, in_specs=in_specs, out_specs=out_specs, check_vma=False,
    )
```

```python
import functools

import jax
import jax.numpy as jnp
from jax import lax
from jax.experimental import pallas as pl
from jax.experimental.pallas import tpu as pltpu
from jax.sharding import PartitionSpec as P

MESH = pl.DeviceIdType.MESH
BF = jnp.bfloat16
F32 = jnp.float32


def low_lanes(shape, half):
    return lax.broadcasted_iota(jnp.int32, shape, 1) < half


def halves(packed, half):
    low = low_lanes(packed.shape, half)
    lead = packed.astype(BF).astype(F32)
    rest = packed - lead
    upper = jnp.where(low, lead, pltpu.roll(rest, half, 1))
    lower = jnp.where(low, pltpu.roll(lead, half, 1), rest)
    return upper.astype(BF), lower.astype(BF)


def kernel(
    n, size, step, half,
    factor, rhs, pattern, out,
    links, a32, ahi, alo, right, w, acc, both, sent, xin, pin, piece, pin_slice, d32, dhi, dlo,
    a_sem, r_sem, l_sem, x_send, x_recv, p_send, p_recv, s_send, s_recv, d_send, d_recv, f_send,
):
    r = lax.axis_index("row")
    c = lax.axis_index("col")
    chunks = size // step
    mid = step // 2
    own = size // n
    bit = own // 2
    diag = r == c
    lower = r > c
    active = r >= c
    helper = (r == n - 1) & (c == n - 2)
    final = (r == n - 1) & (c == n - 1)
    early = n // 2
    from_helper = (c == n - 1) & (r < early)
    passes = lower & (lax.rem(r, 2) == 0) & (r < n - 1) & (c > 0)
    passed = (lax.rem(r, 2) == 1) & (r - 1 > c) & (c > 0)

    def load(k):
        rows = pl.ds(k * step, step)
        return pltpu.make_async_copy(factor.at[0, 0, rows, :], a32.at[rows, :], a_sem.at[k])

    def load_right():
        return pltpu.make_async_copy(rhs.at[0], right, r_sem)

    def load_links():
        return pltpu.make_async_copy(pattern, links, l_sem)

    @pl.when(active)
    def _():
        load_links().start()

    @pl.when(diag | helper)
    def _():
        load_right().start()

    @pl.when(active)
    def _():
        for k in range(chunks):
            load(k).start()

    barrier = pltpu.get_barrier_semaphore()
    for i in range(n):
        @pl.when(diag & (i < r) & ((r < n - 1) | (i == n - 2)))
        def _():
            pl.semaphore_signal(barrier, inc=1, device_id={"col": i}, device_id_type=MESH)

    @pl.when(jnp.logical_not(diag) & jnp.logical_not(from_helper))
    def _():
        pl.semaphore_signal(barrier, inc=1, device_id={"row": c}, device_id_type=MESH)

    @pl.when(passed)
    def _():
        pl.semaphore_signal(barrier, inc=1, device_id={"row": r - 1}, device_id_type=MESH)

    @pl.when(from_helper)
    def _():
        pl.semaphore_signal(
            barrier, inc=1, device_id={"row": n - 1, "col": n - 2}, device_id_type=MESH
        )

    @pl.when(helper)
    def _():
        for j in range(n):
            if j != n - 2:
                pl.semaphore_signal(barrier, inc=1, device_id={"col": j}, device_id_type=MESH)

    block = 64
    part_rows = early * own // 2

    def prepare(k, keep):
        load(k).wait()

        def split(t, carry):
            rows = pl.ds(pl.multiple_of(k * step + t * block, block), block)
            full = a32[rows, :] * keep
            lead = full.astype(BF)
            ahi[rows, :] = lead
            alo[rows, :] = (full - lead.astype(F32)).astype(BF)
            return carry

        lax.fori_loop(0, step // block, split, 0)

    def x_copy(i, m):
        return pltpu.make_async_remote_copy(
            src_ref=sent.at[m], dst_ref=xin.at[m], send_sem=x_send.at[i, m], recv_sem=x_recv.at[m],
            device_id={"row": i}, device_id_type=MESH,
        )

    def p_copy(m):
        return pltpu.make_async_remote_copy(
            src_ref=sent.at[m], dst_ref=pin.at[c, m], send_sem=p_send.at[m], recv_sem=p_recv.at[c, m],
            device_id={"col": jnp.where((r == n - 1) & (c < n - 2), n - 2, r)}, device_id_type=MESH,
        )

    def p_arrival(j, m):
        return pltpu.make_async_remote_copy(
            src_ref=sent.at[m], dst_ref=pin.at[j, m], send_sem=p_send.at[m], recv_sem=p_recv.at[j, m],
            device_id={"col": r}, device_id_type=MESH,
        )

    def f_copy(m):
        return pltpu.make_async_remote_copy(
            src_ref=xin.at[m], dst_ref=xin.at[m], send_sem=f_send.at[m], recv_sem=x_recv.at[m],
            device_id={"row": r + 1}, device_id_type=MESH,
        )

    def d_copy(q):
        rows = pl.ds(q * part_rows, part_rows)
        return pltpu.make_async_remote_copy(
            src_ref=factor.at[0, 0, rows, :], dst_ref=d32.at[rows, :],
            send_sem=d_send.at[q], recv_sem=d_recv.at[q],
            device_id={"col": n - 2}, device_id_type=MESH,
        )

    def e_copy(i):
        return pltpu.make_async_remote_copy(
            src_ref=piece.at[i], dst_ref=pin_slice, send_sem=s_send.at[i], recv_sem=s_recv,
            device_id={"row": i, "col": n - 1}, device_id_type=MESH,
        )

    def s_copy(i):
        return pltpu.make_async_remote_copy(
            src_ref=piece.at[i], dst_ref=pin_slice, send_sem=s_send.at[i], recv_sem=s_recv,
            device_id={"row": i}, device_id_type=MESH,
        )

    def place(value):
        turned = value.T
        out[0, :, :bit] = turned[:half]
        out[0, :, bit:] = turned[half:]

    def weave(k, value):
        first, second = halves(value, half)
        w[k * step:k * step + mid, :] = first
        w[k * step + mid:(k + 1) * step, :] = second

    def product(rows, cols):
        part = jnp.dot(ahi[rows, cols], w[cols, :], preferred_element_type=F32)
        return part + jnp.dot(alo[rows, cols], w[cols, :], preferred_element_type=F32)

    def finish(m, part):
        part = part + pltpu.roll(part, half, 1)
        both[m * step:(m + 1) * step, :] = part
        sent[m] = jnp.where(low_lanes((mid, 2 * half), half), part[:mid], part[mid:])

    def right_chunk(k):
        base = k * step
        return jnp.concatenate(
            [right[:, base:base + mid], right[:, base + mid:base + step]], axis=0
        ).T

    @pl.when(diag | helper)
    def _():
        load_right().wait()

    @pl.when(diag)
    def _():
        for k in range(chunks):
            xin[k] = right_chunk(k)

    @pl.when(active)
    def _():
        load_links().wait()

    @pl.when(diag & (r == 0))
    def _():
        for k in range(chunks):
            weave(k, xin[k])
        for m in range(chunks):
            prepare(m, jnp.float32(1.0))
            finish(m, product(slice(m * step, (m + 1) * step), slice(0, size)))
            if m == 0:
                pl.semaphore_wait(barrier, n - 1)
            for i in range(1, n):
                x_copy(i, m).start()

    @pl.when(active & (r > 0))
    def _():
        keep = jnp.where(diag | (links[r, c] == 1), 1.0, 0.0).astype(F32)

        @pl.when(final)
        def _():
            pl.semaphore_wait(barrier, n - early)
            for q in range(2):
                d_copy(q).start()

        for k in range(chunks):
            prepare(k, keep)

        @pl.when(diag & (r < n - 1))
        def _():
            pl.semaphore_wait(barrier, n - 1)

        @pl.when(lower & jnp.logical_not(helper) & jnp.logical_not(passes))
        def _():
            pl.semaphore_wait(barrier, 1)

        @pl.when(passes)
        def _():
            pl.semaphore_wait(barrier, 2)

        @pl.when(helper)
        def _():
            pl.semaphore_wait(barrier, 1 + early)
            for q in range(2):
                d_copy(q).wait_recv()
            strip = 16

            def split(t, carry):
                rows = pl.ds(pl.multiple_of(t * strip, strip), strip)
                full = d32[rows, :]
                lead = full.astype(BF)
                dhi[rows, :] = lead
                dlo[rows, :] = (full - lead.astype(F32)).astype(BF)
                return carry

            lax.fori_loop(0, early * own // strip, split, 0)

        for k in range(chunks):
            base = k * step

            @pl.when(lower)
            def _():
                x_copy(0, k).wait_recv()

            for j in range(n - 2):
                @pl.when(diag & (j < r) & (r < n - 1))
                def _():
                    p_arrival(j, k).wait_recv()
                    xin[k] = xin[k] - pin[j, k]

            @pl.when(final)
            def _():
                p_arrival(n - 2, k).wait_recv()
                xin[k] = pin[n - 2, k]

            weave(k, xin[k])
            last = k == chunks - 1
            for m in range(chunks):
                rows = slice(m * step, (m + 1) * step)
                part = product(rows, slice(base, base + step))
                if k:
                    part += acc[rows, :]
                if not last:
                    acc[rows, :] = part
                    continue
                finish(m, part)

                @pl.when(helper)
                def _():
                    value = right_chunk(m) - sent[m]
                    for j in range(n - 2):
                        p_arrival(j, m).wait_recv()
                        value = value - pin[j, m]
                    sent[m] = value

                @pl.when(lower)
                def _():
                    p_copy(m).start()

                for i in range(2, n):
                    @pl.when(diag & (i == r + 1))
                    def _():
                        x_copy(i, m).start()

    @pl.when(passes)
    def _():
        for m in range(chunks):
            f_copy(m).start()

    for i in range(1, n):
        @pl.when(diag & (i == r + 1))
        def _():
            for m in range(chunks):
                x_copy(i, m).wait_send()

    for i in range(4, n, 2):
        @pl.when(diag & (i > r + 1) & (r > 0))
        def _():
            for m in range(chunks):
                x_copy(i, m).start()

    @pl.when(helper)
    def _():
        for k in range(chunks):
            weave(k, sent[k])
        for i in range(early):
            rows = slice(i * own, (i + 1) * own)
            part = jnp.dot(dhi[rows, :], w[...], preferred_element_type=F32)
            part += jnp.dot(dlo[rows, :], w[...], preferred_element_type=F32)
            part = part + pltpu.roll(part, half, 1)
            piece[i] = jnp.where(low_lanes((bit, 2 * half), half), part[:bit], part[bit:])
            e_copy(i).start()

    @pl.when(diag)
    def _():
        for i in range(n):
            top = both[i * own:i * own + bit, :]
            bottom = both[i * own + bit:(i + 1) * own, :]
            value = jnp.where(low_lanes((bit, 2 * half), half), top, bottom)
            piece[i] = value

            @pl.when((i != r) if i >= early else ((i != r) & (r < n - 1)))
            def _():
                s_copy(i).start()

            @pl.when(i == r)
            def _():
                place(value)

    @pl.when(jnp.logical_not(diag))
    def _():
        s_copy(0).wait_recv()
        place(pin_slice[...])

    @pl.when(lower)
    def _():
        for m in range(chunks):
            p_copy(m).wait_send()

    for i in range(n):
        @pl.when(diag & (i > r + 1) & ((r == 0) | (i % 2 == 0)))
        def _():
            for m in range(chunks):
                x_copy(i, m).wait_send()

        @pl.when(diag & ((i != r) if i >= early else ((i != r) & (r < n - 1))))
        def _():
            s_copy(i).wait_send()

    @pl.when(passes)
    def _():
        for m in range(chunks):
            f_copy(m).wait_send()

    @pl.when(final)
    def _():
        for q in range(2):
            d_copy(q).wait_send()

    @pl.when(helper)
    def _():
        for i in range(early):
            e_copy(i).wait_send()


def local(n, factor, rhs, pattern):
    size, columns = rhs.shape[1], rhs.shape[2]
    step = 256 if size % 256 == 0 else size
    chunks = size // step
    half = columns
    own = size // n
    dma = pltpu.SemaphoreType.DMA
    solved = pl.pallas_call(
        functools.partial(kernel, n, size, step, half),
        out_shape=jax.ShapeDtypeStruct((1, columns, own), F32),
        in_specs=[
            pl.BlockSpec(memory_space=pltpu.HBM),
            pl.BlockSpec(memory_space=pltpu.HBM),
            pl.BlockSpec(memory_space=pltpu.HBM),
        ],
        out_specs=pl.BlockSpec(memory_space=pltpu.VMEM),
        scratch_shapes=[
            pltpu.SMEM(pattern.shape, jnp.int32),
            pltpu.VMEM((size, size), F32),
            pltpu.VMEM((size, size), BF),
            pltpu.VMEM((size, size), BF),
            pltpu.VMEM((columns, size), F32),
            pltpu.VMEM((size, 2 * half), BF),
            pltpu.VMEM((size, 2 * half), F32),
            pltpu.VMEM((size, 2 * half), F32),
            pltpu.VMEM((chunks, step // 2, 2 * half), F32),
            pltpu.VMEM((chunks, step // 2, 2 * half), F32),
            pltpu.VMEM((n - 1, chunks, step // 2, 2 * half), F32),
            pltpu.VMEM((n, own // 2, 2 * half), F32),
            pltpu.VMEM((own // 2, 2 * half), F32),
            pltpu.VMEM((n // 2 * own, size), F32),
            pltpu.VMEM((n // 2 * own, size), BF),
            pltpu.VMEM((n // 2 * own, size), BF),
            dma((chunks,)),
            dma,
            dma,
            dma((n, chunks)),
            dma((chunks,)),
            dma((chunks,)),
            dma((n - 1, chunks)),
            dma((n,)),
            dma,
            dma((2,)),
            dma((2,)),
            dma((chunks,)),
        ],
        compiler_params=pltpu.CompilerParams(
            collective_id=0, has_side_effects=True, vmem_limit_bytes=40 * 1024 * 1024
        ),
    )(*[pltpu.with_memory_space_constraint(v, pltpu.HBM) for v in (factor, jnp.swapaxes(rhs, 1, 2), pattern)])
    return jnp.swapaxes(solved, 1, 2)


def solution(mesh):
    in_specs = (P(("grp", "row"), "col", None, None), P(("grp", "row"), None, None), P("grp", None))
    out_specs = P(("grp", "col"), "row", None)
    return jax.shard_map(
        functools.partial(local, mesh.shape["row"]),
        mesh=mesh, in_specs=in_specs, out_specs=out_specs, check_vma=False,
    )
```

```python
import functools

import jax
import jax.numpy as jnp
from jax import lax
from jax.experimental import pallas as pl
from jax.experimental.pallas import tpu as pltpu
from jax.sharding import PartitionSpec as P

MESH = pl.DeviceIdType.MESH
BF = jnp.bfloat16
F32 = jnp.float32


def low_lanes(shape, half):
    return lax.broadcasted_iota(jnp.int32, shape, 1) < half


def halves(packed, half):
    low = low_lanes(packed.shape, half)
    lead = packed.astype(BF).astype(F32)
    rest = packed - lead
    upper = jnp.where(low, lead, pltpu.roll(rest, half, 1))
    lower = jnp.where(low, pltpu.roll(lead, half, 1), rest)
    return upper.astype(BF), lower.astype(BF)


def kernel(
    n, size, step, half,
    factor, rhs, pattern, out,
    links, a32, ahi, alo, right, w, acc, both, sent, xin, pin, piece, pin_slice, d32, dhi, dlo,
    a_sem, r_sem, l_sem, x_send, x_recv, p_send, p_recv, s_send, s_recv, d_send, d_recv, f_send,
):
    r = lax.axis_index("row")
    c = lax.axis_index("col")
    chunks = size // step
    mid = step // 2
    own = size // n
    bit = own // 2
    diag = r == c
    lower = r > c
    active = r >= c
    helper = (r == n - 1) & (c == n - 2)
    final = (r == n - 1) & (c == n - 1)
    early = n // 2
    from_helper = (c == n - 1) & (r < early)
    passes = lower & (lax.rem(r, 2) == 0) & (r < n - 1) & (c > 0)
    passed = (lax.rem(r, 2) == 1) & (r - 1 > c) & (c > 0)

    def load(k):
        rows = pl.ds(k * step, step)
        return pltpu.make_async_copy(factor.at[0, 0, rows, :], a32.at[rows, :], a_sem.at[k])

    def load_right():
        return pltpu.make_async_copy(rhs.at[0], right, r_sem)

    def load_links():
        return pltpu.make_async_copy(pattern, links, l_sem)

    barrier = pltpu.get_barrier_semaphore()
    for i in range(n):
        @pl.when(diag & (i < r) & ((r < n - 1) | (i == n - 2)))
        def _():
            pl.semaphore_signal(barrier, inc=1, device_id={"col": i}, device_id_type=MESH)

    @pl.when(jnp.logical_not(diag) & jnp.logical_not(from_helper))
    def _():
        pl.semaphore_signal(barrier, inc=1, device_id={"row": c}, device_id_type=MESH)

    @pl.when(passed)
    def _():
        pl.semaphore_signal(barrier, inc=1, device_id={"row": r - 1}, device_id_type=MESH)

    @pl.when(from_helper)
    def _():
        pl.semaphore_signal(
            barrier, inc=1, device_id={"row": n - 1, "col": n - 2}, device_id_type=MESH
        )

    @pl.when(helper)
    def _():
        for j in range(n):
            if j != n - 2:
                pl.semaphore_signal(barrier, inc=1, device_id={"col": j}, device_id_type=MESH)

    @pl.when(active)
    def _():
        load_links().start()

    @pl.when(diag | helper)
    def _():
        load_right().start()

    @pl.when(active)
    def _():
        for k in range(chunks):
            load(k).start()

    block = 64
    part_rows = early * own // 2

    def prepare(k, keep):
        load(k).wait()

        def split(t, carry):
            rows = pl.ds(pl.multiple_of(k * step + t * block, block), block)
            full = a32[rows, :] * keep
            lead = full.astype(BF)
            ahi[rows, :] = lead
            alo[rows, :] = (full - lead.astype(F32)).astype(BF)
            return carry

        lax.fori_loop(0, step // block, split, 0)

    def x_copy(i, m):
        return pltpu.make_async_remote_copy(
            src_ref=sent.at[m], dst_ref=xin.at[m], send_sem=x_send.at[i, m], recv_sem=x_recv.at[m],
            device_id={"row": i}, device_id_type=MESH,
        )

    def p_copy(m):
        return pltpu.make_async_remote_copy(
            src_ref=sent.at[m], dst_ref=pin.at[c, m], send_sem=p_send.at[m], recv_sem=p_recv.at[c, m],
            device_id={"col": jnp.where((r == n - 1) & (c < n - 2), n - 2, r)}, device_id_type=MESH,
        )

    def p_arrival(j, m):
        return pltpu.make_async_remote_copy(
            src_ref=sent.at[m], dst_ref=pin.at[j, m], send_sem=p_send.at[m], recv_sem=p_recv.at[j, m],
            device_id={"col": r}, device_id_type=MESH,
        )

    def f_copy(m):
        return pltpu.make_async_remote_copy(
            src_ref=xin.at[m], dst_ref=xin.at[m], send_sem=f_send.at[m], recv_sem=x_recv.at[m],
            device_id={"row": r + 1}, device_id_type=MESH,
        )

    def d_copy(q):
        rows = pl.ds(q * part_rows, part_rows)
        return pltpu.make_async_remote_copy(
            src_ref=factor.at[0, 0, rows, :], dst_ref=d32.at[rows, :],
            send_sem=d_send.at[q], recv_sem=d_recv.at[q],
            device_id={"col": n - 2}, device_id_type=MESH,
        )

    def e_copy(i):
        return pltpu.make_async_remote_copy(
            src_ref=piece.at[i], dst_ref=pin_slice, send_sem=s_send.at[i], recv_sem=s_recv,
            device_id={"row": i, "col": n - 1}, device_id_type=MESH,
        )

    def s_copy(i):
        return pltpu.make_async_remote_copy(
            src_ref=piece.at[i], dst_ref=pin_slice, send_sem=s_send.at[i], recv_sem=s_recv,
            device_id={"row": i}, device_id_type=MESH,
        )

    def place(value):
        turned = value.T
        out[0, :, :bit] = turned[:half]
        out[0, :, bit:] = turned[half:]

    def weave(k, value):
        first, second = halves(value, half)
        w[k * step:k * step + mid, :] = first
        w[k * step + mid:(k + 1) * step, :] = second

    def product(rows, cols):
        part = jnp.dot(ahi[rows, cols], w[cols, :], preferred_element_type=F32)
        return part + jnp.dot(alo[rows, cols], w[cols, :], preferred_element_type=F32)

    def finish(m, part):
        part = part + pltpu.roll(part, half, 1)
        both[m * step:(m + 1) * step, :] = part
        sent[m] = jnp.where(low_lanes((mid, 2 * half), half), part[:mid], part[mid:])

    def right_chunk(k):
        base = k * step
        return jnp.concatenate(
            [right[:, base:base + mid], right[:, base + mid:base + step]], axis=0
        ).T

    @pl.when(diag | helper)
    def _():
        load_right().wait()

    @pl.when(diag)
    def _():
        for k in range(chunks):
            xin[k] = right_chunk(k)

    @pl.when(active)
    def _():
        load_links().wait()

    @pl.when(diag & (r == 0))
    def _():
        for k in range(chunks):
            weave(k, xin[k])
        for m in range(chunks):
            prepare(m, jnp.float32(1.0))
            finish(m, product(slice(m * step, (m + 1) * step), slice(0, size)))
            if m == 0:
                pl.semaphore_wait(barrier, n - 1)
            for i in range(1, n):
                x_copy(i, m).start()

    @pl.when(active & (r > 0))
    def _():
        keep = jnp.where(diag | (links[r, c] == 1), 1.0, 0.0).astype(F32)

        @pl.when(final)
        def _():
            pl.semaphore_wait(barrier, n - early)
            for q in range(2):
                d_copy(q).start()

        for k in range(chunks):
            prepare(k, keep)

        @pl.when(diag & (r < n - 1))
        def _():
            pl.semaphore_wait(barrier, n - 1)

        @pl.when(lower & jnp.logical_not(helper) & jnp.logical_not(passes))
        def _():
            pl.semaphore_wait(barrier, 1)

        @pl.when(passes)
        def _():
            pl.semaphore_wait(barrier, 2)

        @pl.when(helper)
        def _():
            pl.semaphore_wait(barrier, 1 + early)
            for q in range(2):
                d_copy(q).wait_recv()
            strip = 16

            def split(t, carry):
                rows = pl.ds(pl.multiple_of(t * strip, strip), strip)
                full = d32[rows, :]
                lead = full.astype(BF)
                dhi[rows, :] = lead
                dlo[rows, :] = (full - lead.astype(F32)).astype(BF)
                return carry

            lax.fori_loop(0, early * own // strip, split, 0)

        for k in range(chunks):
            base = k * step

            @pl.when(lower)
            def _():
                x_copy(0, k).wait_recv()

            for j in range(n - 2):
                @pl.when(diag & (j < r) & (r < n - 1))
                def _():
                    p_arrival(j, k).wait_recv()
                    xin[k] = xin[k] - pin[j, k]

            @pl.when(final)
            def _():
                p_arrival(n - 2, k).wait_recv()
                xin[k] = pin[n - 2, k]

            weave(k, xin[k])
            last = k == chunks - 1
            for m in range(chunks):
                rows = slice(m * step, (m + 1) * step)
                part = product(rows, slice(base, base + step))
                if k:
                    part += acc[rows, :]
                if not last:
                    acc[rows, :] = part
                    continue
                finish(m, part)

                @pl.when(helper)
                def _():
                    value = right_chunk(m) - sent[m]
                    for j in range(n - 2):
                        p_arrival(j, m).wait_recv()
                        value = value - pin[j, m]
                    sent[m] = value

                @pl.when(lower)
                def _():
                    p_copy(m).start()

                for i in range(2, n):
                    @pl.when(diag & (i == r + 1))
                    def _():
                        x_copy(i, m).start()

    @pl.when(passes)
    def _():
        for m in range(chunks):
            f_copy(m).start()

    for i in range(1, n):
        @pl.when(diag & (i == r + 1))
        def _():
            for m in range(chunks):
                x_copy(i, m).wait_send()

    for i in range(4, n, 2):
        @pl.when(diag & (i > r + 1) & (r > 0))
        def _():
            for m in range(chunks):
                x_copy(i, m).start()

    @pl.when(helper)
    def _():
        for k in range(chunks):
            weave(k, sent[k])
        for i in range(early):
            rows = slice(i * own, (i + 1) * own)
            part = jnp.dot(dhi[rows, :], w[...], preferred_element_type=F32)
            part += jnp.dot(dlo[rows, :], w[...], preferred_element_type=F32)
            part = part + pltpu.roll(part, half, 1)
            piece[i] = jnp.where(low_lanes((bit, 2 * half), half), part[:bit], part[bit:])
            e_copy(i).start()

    @pl.when(diag)
    def _():
        for i in range(n):
            top = both[i * own:i * own + bit, :]
            bottom = both[i * own + bit:(i + 1) * own, :]
            value = jnp.where(low_lanes((bit, 2 * half), half), top, bottom)
            piece[i] = value

            @pl.when((i != r) if i >= early else ((i != r) & (r < n - 1)))
            def _():
                s_copy(i).start()

            @pl.when(i == r)
            def _():
                place(value)

    @pl.when(jnp.logical_not(diag))
    def _():
        s_copy(0).wait_recv()
        place(pin_slice[...])

    @pl.when(lower)
    def _():
        for m in range(chunks):
            p_copy(m).wait_send()

    for i in range(n):
        @pl.when(diag & (i > r + 1) & ((r == 0) | (i % 2 == 0)))
        def _():
            for m in range(chunks):
                x_copy(i, m).wait_send()

        @pl.when(diag & ((i != r) if i >= early else ((i != r) & (r < n - 1))))
        def _():
            s_copy(i).wait_send()

    @pl.when(passes)
    def _():
        for m in range(chunks):
            f_copy(m).wait_send()

    @pl.when(final)
    def _():
        for q in range(2):
            d_copy(q).wait_send()

    @pl.when(helper)
    def _():
        for i in range(early):
            e_copy(i).wait_send()


def local(n, factor, rhs, pattern):
    size, columns = rhs.shape[1], rhs.shape[2]
    step = 256 if size % 256 == 0 else size
    chunks = size // step
    half = columns
    own = size // n
    dma = pltpu.SemaphoreType.DMA
    solved = pl.pallas_call(
        functools.partial(kernel, n, size, step, half),
        out_shape=jax.ShapeDtypeStruct((1, columns, own), F32),
        in_specs=[
            pl.BlockSpec(memory_space=pltpu.HBM),
            pl.BlockSpec(memory_space=pltpu.HBM),
            pl.BlockSpec(memory_space=pltpu.HBM),
        ],
        out_specs=pl.BlockSpec(memory_space=pltpu.VMEM),
        scratch_shapes=[
            pltpu.SMEM(pattern.shape, jnp.int32),
            pltpu.VMEM((size, size), F32),
            pltpu.VMEM((size, size), BF),
            pltpu.VMEM((size, size), BF),
            pltpu.VMEM((columns, size), F32),
            pltpu.VMEM((size, 2 * half), BF),
            pltpu.VMEM((size, 2 * half), F32),
            pltpu.VMEM((size, 2 * half), F32),
            pltpu.VMEM((chunks, step // 2, 2 * half), F32),
            pltpu.VMEM((chunks, step // 2, 2 * half), F32),
            pltpu.VMEM((n - 1, chunks, step // 2, 2 * half), F32),
            pltpu.VMEM((n, own // 2, 2 * half), F32),
            pltpu.VMEM((own // 2, 2 * half), F32),
            pltpu.VMEM((n // 2 * own, size), F32),
            pltpu.VMEM((n // 2 * own, size), BF),
            pltpu.VMEM((n // 2 * own, size), BF),
            dma((chunks,)),
            dma,
            dma,
            dma((n, chunks)),
            dma((chunks,)),
            dma((chunks,)),
            dma((n - 1, chunks)),
            dma((n,)),
            dma,
            dma((2,)),
            dma((2,)),
            dma((chunks,)),
        ],
        compiler_params=pltpu.CompilerParams(
            collective_id=0, has_side_effects=True, vmem_limit_bytes=40 * 1024 * 1024
        ),
    )(*[pltpu.with_memory_space_constraint(v, pltpu.HBM) for v in (factor, jnp.swapaxes(rhs, 1, 2), pattern)])
    return jnp.swapaxes(solved, 1, 2)


def solution(mesh):
    in_specs = (P(("grp", "row"), "col", None, None), P(("grp", "row"), None, None), P("grp", None))
    out_specs = P(("grp", "col"), "row", None)
    return jax.shard_map(
        functools.partial(local, mesh.shape["row"]),
        mesh=mesh, in_specs=in_specs, out_specs=out_specs, check_vma=False,
    )
```
